32 devices in a mesh: grid: 16 (over z, y, x), mode: 2 (over core).
Axes of the slice: x: 2, y: 2, z: 4, core: 2. Of those that a mesh axis runs over, the one named last changes fastest.
Arguments:
- field: bfloat16 [288, 96, 8, 128], P('mode', 'grid'), may hold values from -6 to 6
- coupling: bfloat16 [11, 288, 288], P(None, 'mode'), may hold values from -0.0390625 to 0.0390625
- coefs: bfloat16 [11, 96, 8, 128], P(None, 'grid'), may hold values from 0.25 to 2
Outputs:
- applied: bfloat16 [288, 96, 8, 128], P('mode', 'grid')
The draws below stay inside these ranges and needn't reach their ends.
All inputs are finite; a program needn't handle non-finite values.
Results may differ from the reference program's by a relative error of at most 0.005.
Values may be sent and summed in bfloat16 or wider, within the bound.
No kernel may reach another device: no remote copies, remote signals or barrier semaphores. Data moves between devices by JAX's collectives and lax.ppermute only.
A program may use at most 128 MiB of HBM per device.

```python
import math
import jax
import jax.numpy as jnp
from jax import lax

P_SIZE = 288
KL = 11
NY = 8
NZ = 128
NX = 96
N_MODE = 2


def block_levels(rng, shape, shards, smallest, largest):
    loudness, own = 1.0, jax.random.fold_in(rng, 6)
    for position, shards_of in shards:
        heights = jnp.exp(jax.random.uniform(jax.random.fold_in(own, position), (shards_of,), jnp.float32, smallest / len(shards), largest / len(shards)))
        loudness = loudness * jnp.repeat(heights, shape[position] // shards_of).reshape([-1 if axis == position else 1 for axis in range(len(shape))])
    return loudness


def noise(key, dims, scale, reach, split=(), dtype=jnp.bfloat16):
    array = jax.random.normal(key, dims, jnp.float32) * scale
    if len(split) > 0:
        array = block_levels(key, dims, split, -0.22, 0.18) * array
    return jnp.clip(array, min=-reach, max=reach).astype(dtype)


def setup_inputs(seed: int = 0) -> dict:
    key_of = jax.random.split(jax.random.key(seed), 4)
    field = noise(key_of[0], (P_SIZE, NX, NY, NZ), 1.0, 6.0, ((0, 2), (1, 16)))
    coupling = noise(key_of[1], (KL, P_SIZE, P_SIZE), (P_SIZE * KL * 8) ** -0.5, 0.0390625, ((1, 2),))
    coefs = jnp.clip(jnp.exp(math.log(2.0) - 2.0794415 * jax.random.uniform(key_of[2], (KL, NX, NY, NZ), jnp.float32) ** block_levels(key_of[2], (KL, NX, NY, NZ), ((1, 16),), -0.2, 0.2)), 0.25, 2.0).astype(jnp.bfloat16)
    return dict(field=field, coupling=coupling, coefs=coefs)


def operate(values, coef):
    padded = jnp.pad(values, ((0, 0), (1, 1), (1, 1), (1, 1)))
    cpad = jnp.pad(coef, 1)
    centre = padded[:, 1:-1, 1:-1, 1:-1]
    total = jnp.zeros_like(centre)
    shifts = [(slice(2, None), slice(1, -1), slice(1, -1)), (slice(0, -2), slice(1, -1), slice(1, -1)),
              (slice(1, -1), slice(2, None), slice(1, -1)), (slice(1, -1), slice(0, -2), slice(1, -1)),
              (slice(1, -1), slice(1, -1), slice(2, None)), (slice(1, -1), slice(1, -1), slice(0, -2))]
    for sx, sy, sz in shifts:
        face = 0.5 * (coef + cpad[sx, sy, sz])
        total = total + face[None] * (centre - padded[:, sx, sy, sz])
    return total


def reference(field, coupling, coefs):
    block = P_SIZE // N_MODE
    flat = field.reshape(P_SIZE, -1)
    coef_all = coefs.astype(jnp.float32)
    grouped = coupling.reshape(KL, N_MODE, block, P_SIZE).transpose(1, 0, 2, 3)

    def per_block(rows):
        def step(total, inputs):
            weights, coef = inputs
            mixed = jnp.dot(weights, flat, preferred_element_type=jnp.float32).astype(jnp.bfloat16)
            mixed = lax.optimization_barrier(mixed).astype(jnp.float32)
            mixed = mixed.reshape(block, NX, NY, NZ)
            return total + operate(mixed, coef), None

        start = jnp.zeros((block, NX, NY, NZ), jnp.float32)
        total, unused = lax.scan(step, start, (rows, coef_all))
        return total.astype(jnp.bfloat16)

    result = lax.map(per_block, grouped)
    return result.reshape(P_SIZE, NX, NY, NZ)
```

```python
import functools

import jax
import jax.numpy as jnp
from jax import lax
from jax.experimental import pallas as pl
from jax.experimental.pallas import tpu as pltpu
from jax.sharding import PartitionSpec as P

BF16 = jnp.bfloat16
F32 = jnp.float32
SIDES = 6
VMEM_LIMIT = 60 * 2**20


def up(n, m):
    return -(-n // m) * m


def chunk_of(blocks):
    return next(c for c in (3, 2, 1) if blocks % c == 0)


def turn_kernel(f_ref, o_ref, lo_ref, hi_ref, s_ref):
    x = pl.program_id(0)
    modes, _, ny, nz = f_ref.shape
    padded = o_ref.shape[2]
    s_ref[...] = f_ref[:, 0].astype(F32).reshape(modes * ny, nz)
    for y in range(ny):
        rows = s_ref[pl.ds(y, modes, stride=ny), :].astype(BF16)
        if padded > modes:
            rows = jnp.concatenate([rows, jnp.zeros((padded - modes, nz), BF16)], axis=0)
        o_ref[0, y] = rows

    @pl.when(x == 0)
    def _():
        lo_ref[...] = o_ref[0]

    @pl.when(x == pl.num_programs(0) - 1)
    def _():
        hi_ref[...] = o_ref[0]


def turn(field):
    modes, nx, ny, nz = field.shape
    padded = up(modes, 16)
    layer = jax.ShapeDtypeStruct((ny, padded, nz), BF16)
    return pl.pallas_call(
        turn_kernel,
        grid=(nx,),
        in_specs=[pl.BlockSpec((modes, 1, ny, nz), lambda x: (0, x, 0, 0))],
        out_specs=[
            pl.BlockSpec((1, ny, padded, nz), lambda x: (x, 0, 0, 0)),
            pl.BlockSpec((ny, padded, nz), lambda x: (0, 0, 0)),
            pl.BlockSpec((ny, padded, nz), lambda x: (0, 0, 0)),
        ],
        out_shape=[jax.ShapeDtypeStruct((nx, ny, padded, nz), BF16), layer, layer],
        scratch_shapes=[pltpu.VMEM((modes * ny, nz), F32)],
        compiler_params=pltpu.CompilerParams(vmem_limit_bytes=VMEM_LIMIT),
        name="turn",
    )(field)


def main_kernel(sources, *refs):
    w_ref, a_ref = refs[:2]
    f_hbm = refs[2:2 + sources]
    out_hbm, base_hbm = refs[2 + sources:4 + sources]
    f_ref, ta, tb, face, rep, acc, obuf, fsem, osem, bsem = refs[4 + sources:]
    terms, nx, ny, nz = a_ref.shape
    padded = f_ref.shape[3]
    outs = obuf.shape[1]
    step = 16 * chunk_of(padded // 16)
    zero = jnp.zeros((ny, padded, nz), BF16)
    for s in range(sources):
        f_ref[s, 0] = zero
        f_ref[s, nx + 1] = zero

    def load(s, x):
        return pltpu.make_async_copy(f_hbm[s].at[x], f_ref.at[s, x + 1], fsem.at[s, x])

    for x in range(nx):
        for s in range(sources):
            load(s, x).start()
    for s in range(sources):
        load(s, 0).wait()

    def write(x, slot):
        return pltpu.make_async_copy(obuf.at[slot], out_hbm.at[:, x], osem.at[slot])

    def write_base(side):
        return pltpu.make_async_copy(acc.at[side], base_hbm.at[side], bsem.at[side])

    lane = lax.broadcasted_iota(jnp.int32, (ny, nz), 1)
    row = lax.broadcasted_iota(jnp.int32, (ny, nz), 0)

    def faces(x):
        for k in range(terms):
            a = a_ref[k, x].astype(F32)
            before = a_ref[k, jnp.maximum(x - 1, 0)].astype(F32)
            after = a_ref[k, jnp.minimum(x + 1, nx - 1)].astype(F32)
            face[0 * terms + k] = jnp.where(x > 0, 0.5 * (a + before), 0.0)
            face[1 * terms + k] = jnp.where(x < nx - 1, 0.5 * (a + after), 0.0)
            face[2 * terms + k] = 0.5 * (a + jnp.where(row > 0, pltpu.roll(a, 1, 0), 0.0))
            face[3 * terms + k] = 0.5 * (a + jnp.where(row < ny - 1, pltpu.roll(a, ny - 1, 0), 0.0))
            face[4 * terms + k] = 0.5 * (a + jnp.where(lane > 0, pltpu.roll(a, 1, 1), 0.0))
            face[5 * terms + k] = 0.5 * (a + jnp.where(lane < nz - 1, pltpu.roll(a, nz - 1, 1), 0.0))

    def differences(s, x, y, q):
        def at(x, y):
            return f_ref[s, x, y, pl.ds(q, step), :]

        here = at(x + 1, y)
        wide = here.astype(F32)
        lanes = lax.broadcasted_iota(jnp.int32, wide.shape, 1)
        zm = jnp.where(lanes > 0, pltpu.roll(wide, 1, 1), 0.0)
        zp = jnp.where(lanes < nz - 1, pltpu.roll(wide, nz - 1, 1), 0.0)
        return (
            here - at(x, y),
            here - at(x + 2, y),
            here - at(x + 1, y - 1) if y > 0 else here,
            here - at(x + 1, y + 1) if y < ny - 1 else here,
            (wide - zm).astype(BF16),
            (wide - zp).astype(BF16),
        )

    def fill(t_ref, x, y, column):
        for r in range(SIDES * terms):
            rep[r] = jnp.broadcast_to(face[r, pl.ds(y, 1), :], (16, nz)).astype(BF16)
        for s in range(sources):
            for q in range(0, padded, step):
                d = [v.reshape(step // 16, 16, nz) for v in differences(s, x, y, q)]
                for k in range(terms):
                    p = [d[h] * rep[h * terms + k][None] for h in range(SIDES)]
                    t = (p[0] + p[1]) + (p[2] + p[3]) + (p[4] + p[5])
                    at = (s * terms + k) * padded + q
                    t_ref[at:at + step, column * nz:(column + 1) * nz] = t.reshape(step, nz)

    pairs = ny // 2

    def mix(t_ref, side, pair):
        r = jnp.dot(w_ref[...], t_ref[...], preferred_element_type=F32)
        acc[side, pl.ds(2 * pair, outs, stride=ny), :] = r[:, :nz]
        acc[side, pl.ds(2 * pair + 1, outs, stride=ny), :] = r[:, nz:]

    def finish(x, slot):
        obuf[slot] = acc[slot].reshape(outs, ny, nz).astype(BF16)

    bufs = (ta, tb)

    @pl.loop(0, nx)
    def _(x):
        slot = x & 1
        last = jnp.maximum(x - 1, 0)

        @pl.when(x + 1 < nx)
        def _():
            for s in range(sources):
                load(s, x + 1).wait()

        faces(x)
        for pair in range(pairs):
            t_ref, done = bufs[pair % 2], bufs[(pair + 1) % 2]
            if pair == 0:
                mix(done, last & 1, pairs - 1)
            else:
                mix(done, slot, pair - 1)
            for column in range(2):
                fill(t_ref, x, 2 * pair + column, column)
            if pair == 0:
                @pl.when(x > 0)
                def _():
                    @pl.when(x > 2)
                    def _():
                        write(x - 3, 1 - slot).wait()
                    finish(x - 1, 1 - slot)
                    write(x - 1, 1 - slot).start()

                    @pl.when(x == 1)
                    def _():
                        write_base(0).start()
                        write_base(0).wait()

    final = (nx - 1) & 1
    mix(bufs[(pairs - 1) % 2], final, pairs - 1)
    pltpu.make_async_copy(acc.at[final], base_hbm.at[1], bsem.at[1]).start()
    write(nx - 3, final).wait()
    finish(nx - 1, final)
    write(nx - 1, final).start()
    write(nx - 2, 1 - final).wait()
    write(nx - 1, final).wait()
    pltpu.make_async_copy(acc.at[final], base_hbm.at[1], bsem.at[1]).wait()


def main(weights, coefs, fields):
    terms, nx, ny, nz = coefs.shape
    outs = weights.shape[0]
    padded = fields[0].shape[2]
    sources = len(fields)
    depth = sources * terms * padded
    vmem = pl.BlockSpec(memory_space=pltpu.VMEM)
    hbm = pl.BlockSpec(memory_space=pl.ANY)
    return pl.pallas_call(
        functools.partial(main_kernel, sources),
        in_specs=[vmem, vmem] + [hbm] * sources,
        out_specs=[hbm, hbm],
        out_shape=[
            jax.ShapeDtypeStruct((outs, nx, ny, nz), BF16),
            jax.ShapeDtypeStruct((2, outs * ny, nz), F32),
        ],
        scratch_shapes=[
            pltpu.VMEM((sources, nx + 2, ny, padded, nz), BF16),
            pltpu.VMEM((depth, 2 * nz), BF16),
            pltpu.VMEM((depth, 2 * nz), BF16),
            pltpu.VMEM((SIDES * terms, ny, nz), F32),
            pltpu.VMEM((SIDES * terms, 16, nz), BF16),
            pltpu.VMEM((2, outs * ny, nz), F32),
            pltpu.VMEM((2, outs, ny, nz), BF16),
            pltpu.SemaphoreType.DMA((sources, nx)),
            pltpu.SemaphoreType.DMA((2,)),
            pltpu.SemaphoreType.DMA((2,)),
        ],
        compiler_params=pltpu.CompilerParams(vmem_limit_bytes=VMEM_LIMIT),
        cost_estimate=pl.CostEstimate(
            flops=2 * outs * depth * nx * ny * nz, bytes_accessed=8 * 2**20, transcendentals=0
        ),
        name="faces",
    )(weights, coefs, *fields)


def tail_kernel(sources, w_ref, a_ref, ah_ref, base_ref, *refs):
    f_refs = refs[:sources]
    h_refs = refs[sources:2 * sources]
    _, o_ref, t_ref, face, rep, acc = refs[2 * sources:]
    terms, _, ny, nz = a_ref.shape
    padded = t_ref.shape[0] // (sources * terms)
    outs = w_ref.shape[0]
    step = 16 * chunk_of(padded // 16)
    for k in range(terms):
        face[k] = 0.5 * (a_ref[k, 0].astype(F32) + ah_ref[0, k].astype(F32))
    for pair in range(ny // 2):
        for column in range(2):
            y = 2 * pair + column
            for k in range(terms):
                rep[k] = jnp.broadcast_to(face[k, pl.ds(y, 1), :], (16, nz)).astype(BF16)
            for s in range(sources):
                for q in range(0, padded, step):
                    d = f_refs[s][0, y, pl.ds(q, step), :] - h_refs[s][0, y, pl.ds(q, step), :]
                    d = d.reshape(step // 16, 16, nz)
                    for k in range(terms):
                        at = (s * terms + k) * padded + q
                        t_ref[at:at + step, column * nz:(column + 1) * nz] = (d * rep[k][None]).reshape(step, nz)
        r = jnp.dot(w_ref[...], t_ref[...], preferred_element_type=F32)
        acc[pl.ds(2 * pair, outs, stride=ny), :] = r[:, :nz]
        acc[pl.ds(2 * pair + 1, outs, stride=ny), :] = r[:, nz:]
    o_ref[:, 0] = (acc[...] + base_ref[0]).reshape(outs, ny, nz).astype(BF16)


def tail(weights, coefs, coef_halo, base, fields, halos, out):
    terms, nx, ny, nz = coefs.shape
    outs = weights.shape[0]
    padded = fields[0].shape[2]
    sources = len(fields)
    depth = sources * terms * padded
    return pl.pallas_call(
        functools.partial(tail_kernel, sources),
        grid=(2,),
        in_specs=[
            pl.BlockSpec((outs, depth), lambda i: (0, 0)),
            pl.BlockSpec((terms, 1, ny, nz), lambda i: (0, i * (nx - 1), 0, 0)),
            pl.BlockSpec((1, terms, ny, nz), lambda i: (i, 0, 0, 0)),
            pl.BlockSpec((1, outs * ny, nz), lambda i: (i, 0, 0)),
        ]
        + [pl.BlockSpec((1, ny, padded, nz), lambda i: (i * (nx - 1), 0, 0, 0))] * sources
        + [pl.BlockSpec((1, ny, padded, nz), lambda i: (i, 0, 0, 0))] * sources
        + [pl.BlockSpec(memory_space=pl.ANY)],
        out_specs=pl.BlockSpec((outs, 1, ny, nz), lambda i: (0, i * (nx - 1), 0, 0)),
        out_shape=jax.ShapeDtypeStruct(out.shape, BF16),
        input_output_aliases={4 + 2 * sources: 0},
        scratch_shapes=[
            pltpu.VMEM((depth, 2 * nz), BF16),
            pltpu.VMEM((terms, ny, nz), F32),
            pltpu.VMEM((terms, 16, nz), BF16),
            pltpu.VMEM((outs * ny, nz), F32),
        ],
        compiler_params=pltpu.CompilerParams(vmem_limit_bytes=VMEM_LIMIT),
        name="tail",
    )(weights, coefs, coef_halo, base, *fields, *halos, out)


def solution(mesh):
    modes_axis, grid_axis = "mode", "grid"
    sources, bricks = mesh.shape[modes_axis], mesh.shape[grid_axis]

    def around(block):
        found = [block]
        for r in range(1, sources):
            found.append(lax.ppermute(block, modes_axis, [((i + r) % sources, i) for i in range(sources)]))
        return found

    def body(field, coupling, coefs):
        modes = field.shape[0]
        terms, outs, total = coupling.shape
        padded = up(modes, 16)
        forward = [(i, i + 1) for i in range(bricks - 1)]
        backward = [(b, a) for a, b in forward]
        turned, first, last = turn(field)
        below = lax.ppermute(last, grid_axis, forward)
        above = lax.ppermute(first, grid_axis, backward)
        coef_below = lax.ppermute(coefs[:, -1], grid_axis, forward)
        coef_above = lax.ppermute(coefs[:, 0], grid_axis, backward)
        fields = around(turned)

        me = lax.axis_index(modes_axis)
        parts = []
        for r in range(sources):
            part = lax.dynamic_slice_in_dim(coupling, (me + r) % sources * modes, modes, 2)
            parts.append(jnp.pad(part, ((0, 0), (0, 0), (0, padded - modes))))
        weights = jnp.stack(parts).transpose(2, 0, 1, 3).reshape(outs, sources * terms * padded)

        out, base = main(weights, coefs, fields)
        halos = around(jnp.stack([below, above]))
        return tail(weights, coefs, jnp.stack([coef_below, coef_above]), base, fields, halos, out)

    spec = P(modes_axis, grid_axis, None, None)
    return jax.shard_map(
        body,
        mesh=mesh,
        in_specs=(spec, P(None, modes_axis, None), P(None, grid_axis, None, None)),
        out_specs=spec,
        check_vma=False,
    )
```

```python
import functools

import jax
import jax.numpy as jnp
from jax import lax
from jax.experimental import pallas as pl
from jax.experimental.pallas import tpu as pltpu
from jax.sharding import PartitionSpec as P

BF16 = jnp.bfloat16
F32 = jnp.float32
VMEM_LIMIT = 60 * 2**20
MODE, GRID = "mode", "grid"
PARAMS = pltpu.CompilerParams(vmem_limit_bytes=VMEM_LIMIT)
VMEM = pl.BlockSpec(memory_space=pltpu.VMEM)
HBM = pl.BlockSpec(memory_space=pl.ANY)


def block_of(rows):
    return 16 if rows % 16 == 0 else 8


def divisor(n, candidates):
    return next(c for c in candidates if n % c == 0)


def one_hot(count, inner):
    size = count * inner
    r = lax.broadcasted_iota(jnp.int32, (size, size), 0)
    c = lax.broadcasted_iota(jnp.int32, (size, size), 1)
    return (c == lax.rem(r, count) * inner + lax.div(r, count)).astype(F32).astype(BF16)


def permuted(perm, rows):
    return jnp.dot(perm, rows, preferred_element_type=F32).astype(BF16)


def extra_of(terms, ny):
    return ny * -(-terms // ny)


def coef_rows(ref, k, modes, ny):
    return ref.at[k % ny, pl.ds(modes + ny * (k // ny), ny), :]


def turn_kernel(modes, f_ref, a_ref, o_ref, e_ref, d_ref, perm):
    step = pl.program_id(0)
    chunk, nx, ny, nz = f_ref.shape
    terms = a_ref.shape[0]
    block = block_of(chunk)
    odd = lax.rem(lax.axis_index(GRID), 2)
    outer = ((e_ref, (1 - odd) * (nx - 1)), (d_ref, odd * (nx - 1)))

    @pl.when(step == 0)
    def _():
        perm[...] = one_hot(block, ny)
        for out, x in outer:
            for k in range(terms):
                coef_rows(out, k, modes, ny)[...] = a_ref[k, x]

    layers = 2 if nx % 2 == 0 else 1
    for x in range(0, nx, layers):
        for q in range(0, chunk, block):
            wide = jnp.concatenate(
                [f_ref[pl.ds(q, block), x + j].reshape(block * ny, nz) for j in range(layers)], axis=1
            )
            wide = permuted(perm[...], wide)
            for j in range(layers):
                o_ref[x + j, :, pl.ds(q, block), :] = wide[:, j * nz:(j + 1) * nz].reshape(ny, block, nz)
    rows = pl.ds(pl.multiple_of(step * chunk, 8), chunk)
    for out, x in outer:
        out[:, rows, :] = o_ref[x]


def turn(field, coefs):
    modes, nx, ny, nz = field.shape
    chunk = divisor(modes, (48, 72, 64, 32, 16, 8))
    outer = (ny, modes + extra_of(coefs.shape[0], ny), nz)
    block = block_of(chunk)
    whole = pl.BlockSpec(outer, lambda i: (0, 0, 0))
    return pl.pallas_call(
        functools.partial(turn_kernel, modes),
        grid=(modes // chunk,),
        in_specs=[
            pl.BlockSpec((chunk, nx, ny, nz), lambda i: (i, 0, 0, 0)),
            pl.BlockSpec(coefs.shape, lambda i: (0, 0, 0, 0)),
        ],
        out_specs=[pl.BlockSpec((nx, ny, chunk, nz), lambda i: (0, 0, i, 0)), whole, whole],
        scratch_shapes=[pltpu.VMEM((block * ny, block * ny), BF16)],
        out_shape=[
            jax.ShapeDtypeStruct((nx, ny, modes, nz), BF16),
            jax.ShapeDtypeStruct(outer, BF16),
            jax.ShapeDtypeStruct(outer, BF16),
        ],
        compiler_params=PARAMS,
        name="turn",
    )(field, coefs)


def chunk_of(total):
    return divisor(total, (32, 16))


def weights_kernel(c_ref, o_ref):
    terms, _, total = c_ref.shape
    chunk = chunk_of(total)
    pieces = [(k, q) for q in range(0, total, chunk) for k in range(terms)]
    per = 128 // chunk
    for i in range(0, len(pieces), per):
        group = pieces[i:i + per]
        wide = jnp.concatenate([c_ref[k, :, q:q + chunk] for k, q in group], axis=1)
        o_ref[:, i * chunk:i * chunk + len(group) * chunk] = wide


def weights_of(coupling):
    terms, outs, total = coupling.shape
    return pl.pallas_call(
        weights_kernel,
        in_specs=[VMEM],
        out_specs=VMEM,
        out_shape=jax.ShapeDtypeStruct((outs, terms * total), BF16),
        compiler_params=PARAMS,
        name="weights",
    )(coupling)


def layers_kernel(sources, outer, w_ref, a_ref, *refs):
    terms, nx, ny, nz = a_ref.shape
    outs, total = w_ref.shape[0], w_ref.shape[1] // terms
    modes = total // sources
    f_hbm, refs = refs[:sources], refs[sources:]
    if outer:
        even, odd, refs = refs[:sources], refs[sources:2 * sources], refs[2 * sources + 1:]
    out_hbm, f_ref, stage, coef, face, repx, repy, repz, acc, obuf, perm, fsem, osem, *more = refs
    slots = f_ref.shape[0]
    items = repx.shape[0]
    stride = 3 if outer else 1
    block = block_of(outs)
    pairs = ny // 2
    me = lax.axis_index(MODE)
    is_even = lax.rem(lax.axis_index(GRID), 2) == 0

    def place(s):
        return pl.ds(pl.multiple_of(lax.rem(me + s, sources) * modes, 8), modes)

    def load(s, slot, ref):
        return pltpu.make_async_copy(ref, stage.at[slot, :, place(s), :], fsem.at[s, slot])

    layer_of = (None, 0, 1, nx - 2, nx - 1, None) if outer else range(nx)
    if outer:
        ends, csem = more
        copies = []
        for s in range(sources):
            for test, lo, hi in ((is_even, odd[s], even[s]), (~is_even, even[s], odd[s])):
                @pl.when(test)
                def _():
                    load(s, 0, lo.at[:, pl.ds(0, modes), :]).start()
                    load(s, slots - 1, hi.at[:, pl.ds(0, modes), :]).start()
                    if s == 0:
                        for i, ref in ((0, lo), (1, hi)):
                            pltpu.make_async_copy(
                                ref.at[:, pl.ds(modes, ends.shape[2]), :], ends.at[i], csem.at[i]
                            ).start()
    for slot in range(slots):
        if layer_of[slot] is not None:
            for s in range(sources):
                load(s, slot, f_hbm[s].at[layer_of[slot]]).start()

    perm[...] = one_hot(ny, block)
    lane = lax.broadcasted_iota(jnp.int32, (ny, nz), 1)
    row = lax.broadcasted_iota(jnp.int32, (ny, nz), 0)
    for slot in range(slots):
        for y in (0, ny + 1):
            f_ref[slot, y] = jnp.zeros((total, nz), F32)
    if outer:
        for i in range(2):
            pltpu.make_async_copy(even[0].at[:, pl.ds(modes, ends.shape[2]), :], ends.at[i], csem.at[i]).wait()
    for slot in range(slots):
        for k in range(terms):
            if layer_of[slot] is None:
                tile = coef_rows(ends.at[0 if slot == 0 else 1], k, 0, ny)[...]
            else:
                tile = a_ref[k, layer_of[slot]]
            coef[slot, k] = 0.5 * tile.astype(F32)

    def spread(values, y):
        return jnp.broadcast_to(values[pl.ds(y, 1), :], (16, nz)).astype(BF16)

    @pl.loop(0, items)
    def _(i):
        c = 1 + stride * i
        for k in range(terms):
            a = coef[c, k]
            face[0, k] = a + coef[c - 1, k]
            face[1, k] = a + coef[c + 1, k]
            face[2, k] = a + jnp.where(row > 0, pltpu.roll(a, 1, 0), 0.0)
            face[3, k] = a + jnp.where(lane > 0, pltpu.roll(a, 1, 1), 0.0)
            face[4, k] = a + jnp.where(lane < nz - 1, pltpu.roll(a, nz - 1, 1), 0.0)
            face[5, k] = a
        for k in range(terms):
            for y in range(ny):
                repx[i, 0, y, k] = spread(face.at[0, k], y)
                repx[i, 1, y, k] = spread(face.at[1, k], y)
                repy[i, y, k] = spread(face.at[2, k], y)
                repz[i, 0, y, k] = spread(face.at[3, k], y)
                repz[i, 1, y, k] = spread(face.at[4, k], y)
            repy[i, ny, k] = spread(face.at[5, k], ny - 1)

    lanes = lax.broadcasted_iota(jnp.int32, (16, nz), 1)

    def arrive(slot):
        for s in range(sources):
            load(s, slot, f_hbm[s].at[0]).wait()

        @pl.loop(0, ny)
        def _(y):
            f_ref[slot, y + 1] = stage[slot, y].astype(F32)

    def differences(c, y, q):
        def at(c, y):
            return f_ref[c, y + 1, pl.ds(q, 16), :]

        here = at(c, y)
        zm = jnp.where(lanes > 0, pltpu.roll(here, 1, 1), 0.0)
        zp = jnp.where(lanes < nz - 1, pltpu.roll(here, nz - 1, 1), 0.0)
        others = (at(c - 1, y), at(c + 1, y), at(c, y - 1), at(c, y + 1), zm, zp)
        return [(here - v).astype(BF16) for v in others]

    def rows_of(i, c, y, q):
        ds = [differences(c, y, q + g) for g in range(0, chunk_of(total), 16)]
        rows = []
        for k in range(terms):
            w = (repx[i, 0, y, k], repx[i, 1, y, k], repy[i, y, k], repy[i, y + 1, k], repz[i, 0, y, k], repz[i, 1, y, k])
            for d in ds:
                p = [u * v for u, v in zip(d, w)]
                rows.append((p[0] + p[1]) + (p[2] + p[3]) + (p[4] + p[5]))
        return rows

    def mix(i, c, slot, pair):
        sides = ([], [])
        for q in range(0, total, chunk_of(total)):
            for column in range(2):
                sides[column].extend(rows_of(i, c, 2 * pair + column, q))
        t = jnp.concatenate([jnp.concatenate(side, axis=0) for side in sides], axis=1)
        r = jnp.dot(w_ref[...], t, preferred_element_type=F32).astype(BF16)
        acc[2 * pair] = r[:, :nz]
        acc[2 * pair + 1] = r[:, nz:]

    def finish(slot):
        for p in range(0, outs, block):
            rows = acc[:, pl.ds(p, block), :].reshape(ny * block, nz)
            obuf[slot, pl.ds(p, block)] = permuted(perm[...], rows).reshape(block, ny, nz)

    def write(i, slot):
        x = i * (nx - 1) if outer else i + 1
        return pltpu.make_async_copy(obuf.at[slot], out_hbm.at[:, x], osem.at[slot])

    unroll = 2 if pairs % 2 == 0 else 1

    @pl.loop(0, items)
    def _(i):
        slot = i & 1
        c = 1 + stride * i
        if outer:
            for j in range(3):
                arrive(3 * i + j)
        else:
            @pl.when(i == 0)
            def _():
                arrive(0)
                arrive(1)
            arrive(i + 2)

        @pl.loop(0, pairs // unroll)
        def _(n):
            for j in range(unroll):
                mix(i, c, slot, unroll * n + j)

        @pl.when(i > 1)
        def _():
            write(i - 2, slot).wait()

        finish(slot)
        write(i, slot).start()

    for i in range(max(items - 2, 0), items):
        write(i, i & 1).wait()


def layers(weights, coefs, fields, halos=None, out=None):
    outer = halos is not None
    terms, nx, ny, nz = coefs.shape
    outs, depth = weights.shape
    total = depth // terms
    sources = len(fields)
    block = block_of(outs)
    items = 2 if outer else nx - 2
    slots = 6 if outer else nx
    shape = jax.ShapeDtypeStruct((outs, nx, ny, nz), BF16)
    operands = [weights, coefs, *fields] + ([*halos[0], *halos[1], out] if outer else [])
    more = []
    if outer:
        more = [pltpu.VMEM((2, ny, extra_of(terms, ny), nz), BF16), pltpu.SemaphoreType.DMA((2,))]
    return pl.pallas_call(
        functools.partial(layers_kernel, sources, outer),
        in_specs=[VMEM, VMEM] + [HBM] * (len(operands) - 2),
        out_specs=HBM,
        out_shape=shape,
        input_output_aliases={len(operands) - 1: 0} if outer else {},
        scratch_shapes=[
            pltpu.VMEM((slots, ny + 2, total, nz), F32),
            pltpu.VMEM((slots, ny, total, nz), BF16),
            pltpu.VMEM((slots, terms, ny, nz), F32),
            pltpu.VMEM((6, terms, ny, nz), F32),
            pltpu.VMEM((items, 2, ny, terms, 16, nz), BF16),
            pltpu.VMEM((items, ny + 1, terms, 16, nz), BF16),
            pltpu.VMEM((items, 2, ny, terms, 16, nz), BF16),
            pltpu.VMEM((ny, outs, nz), BF16),
            pltpu.VMEM((2, outs, ny, nz), BF16),
            pltpu.VMEM((block * ny, block * ny), BF16),
            pltpu.SemaphoreType.DMA((sources, slots)),
            pltpu.SemaphoreType.DMA((2,)),
            *more,
        ],
        compiler_params=PARAMS,
        cost_estimate=pl.CostEstimate(
            flops=2 * outs * depth * items * ny * nz, bytes_accessed=6 * 2**20, transcendentals=0
        ),
        name="outer" if outer else "inner",
    )(*operands)


def solution(mesh):
    sources, bricks = mesh.shape[MODE], mesh.shape[GRID]

    def around(block):
        found = [block]
        for r in range(1, sources):
            found.append(lax.ppermute(block, MODE, [((i + r) % sources, i) for i in range(sources)]))
        return found

    def exchange(block, offset):
        pairs = [(i, i + 1) for i in range(offset, bricks - 1, 2)]
        return lax.ppermute(block, GRID, pairs + [(b, a) for a, b in pairs])

    def body(field, coupling, coefs):
        turned, even_out, odd_out = turn(field, coefs)
        even_in, odd_in = exchange(even_out, 0), exchange(odd_out, 1)
        fields = around(turned)
        weights = weights_of(coupling)
        out = layers(weights, coefs, fields)
        even_in, odd_in, out = lax.optimization_barrier((even_in, odd_in, out))
        return layers(weights, coefs, fields, (around(even_in), around(odd_in)), out)

    spec = P(MODE, GRID, None, None)
    return jax.shard_map(
        body,
        mesh=mesh,
        in_specs=(spec, P(None, MODE, None), P(None, GRID, None, None)),
        out_specs=spec,
        check_vma=False,
    )
```

```python
import functools

import jax
import jax.numpy as jnp
from jax import lax
from jax.experimental import pallas as pl
from jax.experimental.pallas import tpu as pltpu
from jax.sharding import PartitionSpec as P

BF16 = jnp.bfloat16
F32 = jnp.float32
VMEM_LIMIT = 60 * 2**20
MODE, GRID = "mode", "grid"
PARAMS = pltpu.CompilerParams(vmem_limit_bytes=VMEM_LIMIT)
VMEM = pl.BlockSpec(memory_space=pltpu.VMEM)
HBM = pl.BlockSpec(memory_space=pl.ANY)


def block_of(rows):
    return 16 if rows % 16 == 0 else 8


def divisor(n, candidates):
    return next(c for c in candidates if n % c == 0)


def one_hot(count, inner):
    size = count * inner
    r = lax.broadcasted_iota(jnp.int32, (size, size), 0)
    c = lax.broadcasted_iota(jnp.int32, (size, size), 1)
    return (c == lax.rem(r, count) * inner + lax.div(r, count)).astype(F32).astype(BF16)


def permuted(perm, rows):
    return jnp.dot(perm, rows, preferred_element_type=F32).astype(BF16)


def extra_of(terms, ny):
    return ny * -(-terms // ny)


def coef_rows(ref, k, modes, ny):
    return ref.at[k % ny, pl.ds(modes + ny * (k // ny), ny), :]


def turn_kernel(modes, f_ref, a_ref, o_ref, e_ref, d_ref, *more):
    send, perm = more[:-1], more[-1]
    step = pl.program_id(0)
    chunk, nx, ny, nz = f_ref.shape
    terms = a_ref.shape[0]
    block = block_of(chunk)
    odd = lax.rem(lax.axis_index(GRID), 2)
    outer = ((e_ref, (1 - odd) * (nx - 1)), (d_ref, odd * (nx - 1)))

    @pl.when(step == 0)
    def _():
        perm[...] = one_hot(block, ny)
        for out, x in outer:
            for k in range(terms):
                coef_rows(out, k, modes, ny)[...] = a_ref[k, x]

    layers = 2 if nx % 2 == 0 else 1
    for x in range(0, nx, layers):
        for q in range(0, chunk, block):
            wide = jnp.concatenate(
                [f_ref[pl.ds(q, block), x + j].reshape(block * ny, nz) for j in range(layers)], axis=1
            )
            wide = permuted(perm[...], wide)
            for j in range(layers):
                o_ref[x + j, :, pl.ds(q, block), :] = wide[:, j * nz:(j + 1) * nz].reshape(ny, block, nz)
    rows = pl.ds(pl.multiple_of(step * chunk, 8), chunk)
    for out, x in outer:
        out[:, rows, :] = o_ref[x]
    for out in send:
        count = out.shape[0]
        out[...] = o_ref[pl.ds((1 - lax.axis_index(MODE)) * (nx - count), count)]


def turn(field, coefs, sent=0):
    modes, nx, ny, nz = field.shape
    chunk = divisor(modes, (48, 72, 64, 32, 16, 8))
    outer = (ny, modes + extra_of(coefs.shape[0], ny), nz)
    block = block_of(chunk)
    whole = pl.BlockSpec(outer, lambda i: (0, 0, 0))
    return pl.pallas_call(
        functools.partial(turn_kernel, modes),
        grid=(modes // chunk,),
        in_specs=[
            pl.BlockSpec((chunk, nx, ny, nz), lambda i: (i, 0, 0, 0)),
            pl.BlockSpec(coefs.shape, lambda i: (0, 0, 0, 0)),
        ],
        out_specs=[pl.BlockSpec((nx, ny, chunk, nz), lambda i: (0, 0, i, 0)), whole, whole]
        + [pl.BlockSpec((sent, ny, chunk, nz), lambda i: (0, 0, i, 0))] * (sent > 0),
        scratch_shapes=[pltpu.VMEM((block * ny, block * ny), BF16)],
        out_shape=[
            jax.ShapeDtypeStruct((nx, ny, modes, nz), BF16),
            jax.ShapeDtypeStruct(outer, BF16),
            jax.ShapeDtypeStruct(outer, BF16),
        ]
        + [jax.ShapeDtypeStruct((sent, ny, modes, nz), BF16)] * (sent > 0),
        compiler_params=PARAMS,
        name="turn",
    )(field, coefs)


def chunk_of(total):
    return divisor(total, (32, 16))


def weights_kernel(c_ref, o_ref):
    terms, _, total = c_ref.shape
    chunk = chunk_of(total)
    pieces = [(k, q) for q in range(0, total, chunk) for k in range(terms)]
    per = 128 // chunk
    for i in range(0, len(pieces), per):
        group = pieces[i:i + per]
        wide = jnp.concatenate([c_ref[k, :, q:q + chunk] for k, q in group], axis=1)
        o_ref[:, i * chunk:i * chunk + len(group) * chunk] = wide


def weights_of(coupling):
    terms, outs, total = coupling.shape
    return pl.pallas_call(
        weights_kernel,
        in_specs=[VMEM],
        out_specs=VMEM,
        out_shape=jax.ShapeDtypeStruct((outs, terms * total), BF16),
        compiler_params=PARAMS,
        name="weights",
    )(coupling)


class Engine:
    def __init__(self, w_refs, terms, f_ref, stage, coef, face, repx, repy, repz, acc, obuf, perm):
        self.w_refs, self.terms = w_refs, terms
        self.f_ref, self.stage, self.coef, self.face = f_ref, stage, coef, face
        self.repx, self.repy, self.repz = repx, repy, repz
        self.acc, self.obuf, self.perm = acc, obuf, perm
        _, self.ny, self.total, self.nz = stage.shape
        self.outs = acc.shape[1]
        self.block = block_of(self.outs // len(w_refs))

    def prepare(self):
        self.perm[...] = one_hot(self.ny, self.block)
        for slot in range(self.f_ref.shape[0]):
            for y in (0, self.ny + 1):
                self.f_ref[slot, y] = jnp.zeros((self.total, self.nz), F32)

    def spread(self, at, y):
        return jnp.broadcast_to(self.face[at + (pl.ds(y, 1), slice(None))], (16, self.nz)).astype(BF16)

    def faces(self, i, c):
        ny, nz, terms, face = self.ny, self.nz, self.terms, self.face
        lane = lax.broadcasted_iota(jnp.int32, (ny, nz), 1)
        row = lax.broadcasted_iota(jnp.int32, (ny, nz), 0)
        for k in range(terms):
            a = self.coef[c, k]
            face[0, k] = a + self.coef[c - 1, k]
            face[1, k] = a + self.coef[c + 1, k]
            face[2, k] = a + jnp.where(row > 0, pltpu.roll(a, 1, 0), 0.0)
            face[3, k] = a + jnp.where(lane > 0, pltpu.roll(a, 1, 1), 0.0)
            face[4, k] = a + jnp.where(lane < nz - 1, pltpu.roll(a, nz - 1, 1), 0.0)
            face[5, k] = a
        for k in range(terms):
            for y in range(ny):
                self.repx[i, 0, y, k] = self.spread((0, k), y)
                self.repx[i, 1, y, k] = self.spread((1, k), y)
                self.repy[i, y, k] = self.spread((2, k), y)
                self.repz[i, 0, y, k] = self.spread((3, k), y)
                self.repz[i, 1, y, k] = self.spread((4, k), y)
            self.repy[i, ny, k] = self.spread((5, k), ny - 1)

    def widen(self, slot):
        @pl.loop(0, self.ny)
        def _(y):
            self.f_ref[slot, y + 1] = self.stage[slot, y].astype(F32)

    def differences(self, c, y, q):
        lanes = lax.broadcasted_iota(jnp.int32, (16, self.nz), 1)

        def at(c, y):
            return self.f_ref[c, y + 1, pl.ds(q, 16), :]

        here = at(c, y)
        zm = jnp.where(lanes > 0, pltpu.roll(here, 1, 1), 0.0)
        zp = jnp.where(lanes < self.nz - 1, pltpu.roll(here, self.nz - 1, 1), 0.0)
        others = (at(c - 1, y), at(c + 1, y), at(c, y - 1), at(c, y + 1), zm, zp)
        return [(here - v).astype(BF16) for v in others]

    def rows_of(self, i, c, y, q):
        ds = [self.differences(c, y, q + g) for g in range(0, chunk_of(self.total), 16)]
        x, z = self.repx, self.repz
        rows = []
        for k in range(self.terms):
            w = (x[i, 0, y, k], x[i, 1, y, k], self.repy[i, y, k], self.repy[i, y + 1, k], z[i, 0, y, k], z[i, 1, y, k])
            for d in ds:
                p = [u * v for u, v in zip(d, w)]
                rows.append((p[0] + p[1]) + (p[2] + p[3]) + (p[4] + p[5]))
        return rows

    def pair(self, i, c, n):
        sides = ([], [])
        for q in range(0, self.total, chunk_of(self.total)):
            for column in range(2):
                sides[column].extend(self.rows_of(i, c, 2 * n + column, q))
        t = jnp.concatenate([jnp.concatenate(side, axis=0) for side in sides], axis=1)
        w = jnp.concatenate([w_ref[...] for w_ref in self.w_refs], axis=0)
        r = jnp.dot(w, t, preferred_element_type=F32).astype(BF16)
        self.acc[2 * n] = r[:, :self.nz]
        self.acc[2 * n + 1] = r[:, self.nz:]

    def layer(self, i, c):
        pairs = self.ny // 2
        unroll = 2 if pairs % 2 == 0 else 1

        @pl.loop(0, pairs // unroll)
        def _(n):
            for j in range(unroll):
                self.pair(i, c, unroll * n + j)

    def finish(self, slot):
        for p in range(0, self.outs, self.block):
            rows = self.acc[:, pl.ds(p, self.block), :].reshape(self.ny * self.block, self.nz)
            rows = permuted(self.perm[...], rows)
            self.obuf[slot, pl.ds(p, self.block)] = rows.reshape(self.block, self.ny, self.nz)


def engine_scratch(slots, items, terms, ny, nz, total, outs, block):
    return [
        pltpu.VMEM((slots, ny + 2, total, nz), F32),
        pltpu.VMEM((slots, ny, total, nz), BF16),
        pltpu.VMEM((slots, terms, ny, nz), F32),
        pltpu.VMEM((6, terms, ny, nz), F32),
        pltpu.VMEM((items, 2, ny, terms, 16, nz), BF16),
        pltpu.VMEM((items, ny + 1, terms, 16, nz), BF16),
        pltpu.VMEM((items, 2, ny, terms, 16, nz), BF16),
        pltpu.VMEM((ny, outs, nz), BF16),
        pltpu.VMEM((2, outs, ny, nz), BF16),
        pltpu.VMEM((block * ny, block * ny), BF16),
    ]


def half_kernel(outer, w_ref, w2_ref, a_ref, own, other, *refs):
    terms, nx, ny, nz = a_ref.shape
    total = w_ref.shape[1] // terms
    modes, outs = total // 2, w_ref.shape[0]
    half = nx // 2
    me = lax.axis_index(MODE)
    if outer:
        halos, refs = refs[:4], refs[5:]
    out_hbm, give_hbm, *refs = refs
    engine = Engine((w_ref, w2_ref), terms, *refs[:10])
    fsem, osem, *more = refs[10:]
    stage, coef = engine.stage, engine.coef
    slots, items = coef.shape[0], engine.repx.shape[0]
    first = me * (half - 1)

    def load(s, slot, ref):
        rows = pl.ds(pl.multiple_of(lax.rem(me + s, 2) * modes, 8), modes)
        return pltpu.make_async_copy(ref, stage.at[slot, :, rows, :], fsem.at[s, slot])

    if outer:
        ends, csem = more
        even, odd = halos[:2], halos[2:]
        takes_odd = (me == 0) == (lax.rem(lax.axis_index(GRID), 2) == 0)
        layer_of = [(1 - me + j, me * (nx - 2) + j) for j in range(2)]
        end = 2 * me
        for test, halo in ((takes_odd, odd), (jnp.logical_not(takes_odd), even)):
            @pl.when(test)
            def _():
                for s in range(2):
                    load(s, end, halo[s].at[:, pl.ds(0, modes), :]).start()
                pltpu.make_async_copy(halo[0].at[:, pl.ds(modes, ends.shape[1]), :], ends, csem).start()
    else:
        layer_of = [(slot, first + slot) for slot in range(slots)]
    for slot, x in layer_of:
        load(0, slot, own.at[x]).start()
        load(1, slot, other.at[x - first]).start()
    engine.prepare()
    for slot, x in layer_of:
        for k in range(terms):
            coef[slot, k] = 0.5 * a_ref[k, x].astype(F32)
    if outer:
        pltpu.make_async_copy(even[0].at[:, pl.ds(modes, ends.shape[1]), :], ends, csem).wait()
        for k in range(terms):
            coef[end, k] = 0.5 * coef_rows(ends, k, 0, ny)[...].astype(F32)

    @pl.loop(0, items)
    def _(i):
        engine.faces(i, i + 1)

    def arrive(slot):
        for s in range(2):
            load(s, slot, own.at[0]).wait()
        engine.widen(slot)

    def writes(i, slot):
        x = me * (nx - 1) if outer else first + i + 1
        return (
            pltpu.make_async_copy(engine.obuf.at[slot, pl.ds(0, outs)], out_hbm.at[:, x], osem.at[0, slot]),
            pltpu.make_async_copy(engine.obuf.at[slot, pl.ds(outs, outs)], give_hbm.at[:, i], osem.at[1, slot]),
        )

    arrive(0)
    arrive(1)

    @pl.loop(0, items)
    def _(i):
        slot = i & 1
        arrive(i + 2)
        engine.layer(i, i + 1)

        @pl.when(i > 1)
        def _():
            for copy in writes(i - 2, slot):
                copy.wait()

        engine.finish(slot)
        for copy in writes(i, slot):
            copy.start()

    for i in range(max(items - 2, 0), items):
        for copy in writes(i, i & 1):
            copy.wait()


def half_layers(weights, coefs, own, other, halos=(), out=()):
    outer = len(halos) > 0
    terms, nx, ny, nz = coefs.shape
    outs, depth = weights[0].shape
    total = depth // terms
    items = 1 if outer else nx // 2 - 1
    slots = items + 2
    block = block_of(outs)
    operands = [*weights, coefs, own, other, *halos, *out]
    more = []
    if outer:
        more = [pltpu.VMEM((ny, extra_of(terms, ny), nz), BF16), pltpu.SemaphoreType.DMA]
    return pl.pallas_call(
        functools.partial(half_kernel, outer),
        in_specs=[VMEM, VMEM, VMEM] + [HBM] * (len(operands) - 3),
        out_specs=[HBM, HBM],
        out_shape=[
            jax.ShapeDtypeStruct((outs, nx, ny, nz), BF16),
            jax.ShapeDtypeStruct((outs, items, ny, nz), BF16),
        ],
        input_output_aliases={len(operands) - 1: 0} if outer else {},
        scratch_shapes=[
            *engine_scratch(slots, items, terms, ny, nz, total, 2 * outs, block),
            pltpu.SemaphoreType.DMA((2, slots)),
            pltpu.SemaphoreType.DMA((2, 2)),
            *more,
        ],
        compiler_params=PARAMS,
        cost_estimate=pl.CostEstimate(
            flops=4 * outs * depth * items * ny * nz, bytes_accessed=5 * 2**20, transcendentals=0
        ),
        name="outer" if outer else "inner",
    )(*operands)


def join_kernel(a_ref, b_ref, _, out_hbm, sem):
    nx, inner = out_hbm.shape[1], a_ref.shape[1]
    partner = 1 - lax.axis_index(MODE)
    first = 1 + partner * inner
    copies = [
        pltpu.make_async_copy(a_ref, out_hbm.at[:, pl.ds(first, inner)], sem.at[0]),
        pltpu.make_async_copy(b_ref, out_hbm.at[:, pl.ds(partner * (nx - 1), 1)], sem.at[1]),
    ]
    for copy in copies:
        copy.start()
    for copy in copies:
        copy.wait()


def join(inner, outer, out):
    return pl.pallas_call(
        join_kernel,
        in_specs=[VMEM, VMEM, HBM],
        out_specs=HBM,
        out_shape=jax.ShapeDtypeStruct(out.shape, BF16),
        input_output_aliases={2: 0},
        scratch_shapes=[pltpu.SemaphoreType.DMA((2,))],
        compiler_params=PARAMS,
        name="join",
    )(inner, outer, out)


def layers_kernel(sources, outer, w_ref, a_ref, *refs):
    terms, nx, ny, nz = a_ref.shape
    outs, total = w_ref.shape[0], w_ref.shape[1] // terms
    modes = total // sources
    f_hbm, refs = refs[:sources], refs[sources:]
    if outer:
        even, odd, refs = refs[:sources], refs[sources:2 * sources], refs[2 * sources + 1:]
    out_hbm, *refs = refs
    engine = Engine((w_ref,), terms, *refs[:10])
    fsem, osem, *more = refs[10:]
    stage, coef, obuf = engine.stage, engine.coef, engine.obuf
    slots, items = coef.shape[0], engine.repx.shape[0]
    stride = 3 if outer else 1
    me = lax.axis_index(MODE)
    is_even = lax.rem(lax.axis_index(GRID), 2) == 0

    def place(s):
        return pl.ds(pl.multiple_of(lax.rem(me + s, sources) * modes, 8), modes)

    def load(s, slot, ref):
        return pltpu.make_async_copy(ref, stage.at[slot, :, place(s), :], fsem.at[s, slot])

    layer_of = (None, 0, 1, nx - 2, nx - 1, None) if outer else range(nx)
    if outer:
        ends, csem = more
        copies = []
        for s in range(sources):
            for test, lo, hi in ((is_even, odd[s], even[s]), (~is_even, even[s], odd[s])):
                @pl.when(test)
                def _():
                    load(s, 0, lo.at[:, pl.ds(0, modes), :]).start()
                    load(s, slots - 1, hi.at[:, pl.ds(0, modes), :]).start()
                    if s == 0:
                        for i, ref in ((0, lo), (1, hi)):
                            pltpu.make_async_copy(
                                ref.at[:, pl.ds(modes, ends.shape[2]), :], ends.at[i], csem.at[i]
                            ).start()
    for slot in range(slots):
        if layer_of[slot] is not None:
            for s in range(sources):
                load(s, slot, f_hbm[s].at[layer_of[slot]]).start()

    engine.prepare()
    if outer:
        for i in range(2):
            pltpu.make_async_copy(even[0].at[:, pl.ds(modes, ends.shape[2]), :], ends.at[i], csem.at[i]).wait()
    for slot in range(slots):
        for k in range(terms):
            if layer_of[slot] is None:
                tile = coef_rows(ends.at[0 if slot == 0 else 1], k, 0, ny)[...]
            else:
                tile = a_ref[k, layer_of[slot]]
            coef[slot, k] = 0.5 * tile.astype(F32)

    @pl.loop(0, items)
    def _(i):
        engine.faces(i, 1 + stride * i)

    def arrive(slot):
        for s in range(sources):
            load(s, slot, f_hbm[s].at[0]).wait()
        engine.widen(slot)

    def write(i, slot):
        x = i * (nx - 1) if outer else i + 1
        return pltpu.make_async_copy(obuf.at[slot], out_hbm.at[:, x], osem.at[slot])

    @pl.loop(0, items)
    def _(i):
        slot = i & 1
        if outer:
            for j in range(3):
                arrive(3 * i + j)
        else:
            @pl.when(i == 0)
            def _():
                arrive(0)
                arrive(1)
            arrive(i + 2)

        engine.layer(i, 1 + stride * i)

        @pl.when(i > 1)
        def _():
            write(i - 2, slot).wait()

        engine.finish(slot)
        write(i, slot).start()

    for i in range(max(items - 2, 0), items):
        write(i, i & 1).wait()


def layers(weights, coefs, fields, halos=None, out=None):
    outer = halos is not None
    terms, nx, ny, nz = coefs.shape
    outs, depth = weights.shape
    total = depth // terms
    sources = len(fields)
    block = block_of(outs)
    items = 2 if outer else nx - 2
    slots = 6 if outer else nx
    shape = jax.ShapeDtypeStruct((outs, nx, ny, nz), BF16)
    operands = [weights, coefs, *fields] + ([*halos[0], *halos[1], out] if outer else [])
    more = []
    if outer:
        more = [pltpu.VMEM((2, ny, extra_of(terms, ny), nz), BF16), pltpu.SemaphoreType.DMA((2,))]
    return pl.pallas_call(
        functools.partial(layers_kernel, sources, outer),
        in_specs=[VMEM, VMEM] + [HBM] * (len(operands) - 2),
        out_specs=HBM,
        out_shape=shape,
        input_output_aliases={len(operands) - 1: 0} if outer else {},
        scratch_shapes=[
            *engine_scratch(slots, items, terms, ny, nz, total, outs, block),
            pltpu.SemaphoreType.DMA((sources, slots)),
            pltpu.SemaphoreType.DMA((2,)),
            *more,
        ],
        compiler_params=PARAMS,
        cost_estimate=pl.CostEstimate(
            flops=2 * outs * depth * items * ny * nz, bytes_accessed=6 * 2**20, transcendentals=0
        ),
        name="outer" if outer else "inner",
    )(*operands)


def solution(mesh):
    sources, bricks = mesh.shape[MODE], mesh.shape[GRID]

    def around(block):
        found = [block]
        for r in range(1, sources):
            found.append(lax.ppermute(block, MODE, [((i + r) % sources, i) for i in range(sources)]))
        return found

    def exchange(block, offset):
        pairs = [(i, i + 1) for i in range(offset, bricks - 1, 2)]
        return lax.ppermute(block, GRID, pairs + [(b, a) for a, b in pairs])

    def halves(field, coupling, coefs):
        def swap(block):
            return lax.ppermute(block, MODE, [(0, 1), (1, 0)])

        weights = weights_of(coupling)
        weights, field = lax.optimization_barrier((weights, field))
        weights = (weights, swap(weights))
        turned, even_out, odd_out, send = turn(field, coefs, coefs.shape[1] // 2 + 1)
        even_in, odd_in = exchange(even_out, 0), exchange(odd_out, 1)
        other = swap(send)
        out, give = half_layers(weights, coefs, turned, other)
        even_in, odd_in, out, give = lax.optimization_barrier((even_in, odd_in, out, give))
        inner = swap(give)
        halos = (even_in, swap(even_in), odd_in, swap(odd_in))
        out, give = half_layers(weights, coefs, turned, other, halos, (out,))
        return join(inner, swap(give), out)

    def body(field, coupling, coefs):
        if sources == 2 and coefs.shape[1] % 2 == 0 and coefs.shape[1] >= 4:
            return halves(field, coupling, coefs)
        turned, even_out, odd_out = turn(field, coefs)
        even_in, odd_in = exchange(even_out, 0), exchange(odd_out, 1)
        fields = around(turned)
        weights = weights_of(coupling)
        out = layers(weights, coefs, fields)
        even_in, odd_in, out = lax.optimization_barrier((even_in, odd_in, out))
        return layers(weights, coefs, fields, (around(even_in), around(odd_in)), out)

    spec = P(MODE, GRID, None, None)
    return jax.shard_map(
        body,
        mesh=mesh,
        in_specs=(spec, P(None, MODE, None), P(None, GRID, None, None)),
        out_specs=spec,
        check_vma=False,
    )
```

```python
import functools
import math

import jax
import jax.numpy as jnp
from jax import lax
from jax.experimental import pallas as pl
from jax.experimental.pallas import tpu as pltpu
from jax.sharding import PartitionSpec as P

BF16 = jnp.bfloat16
F32 = jnp.float32
MODE, GRID = "mode", "grid"


def grant(*parts):
    size = sum(math.prod(p.shape) * jnp.dtype(p.dtype).itemsize for p in parts)
    return pltpu.CompilerParams(vmem_limit_bytes=min(size + 10 * 2**20, 60 * 2**20))


VMEM = pl.BlockSpec(memory_space=pltpu.VMEM)
HBM = pl.BlockSpec(memory_space=pl.ANY)


def block_of(rows):
    return 16 if rows % 16 == 0 else 8


def divisor(n, candidates):
    return next(c for c in candidates if n % c == 0)


def one_hot(count, inner):
    size = count * inner
    r = lax.broadcasted_iota(jnp.int32, (size, size), 0)
    c = lax.broadcasted_iota(jnp.int32, (size, size), 1)
    return (c == lax.rem(r, count) * inner + lax.div(r, count)).astype(F32).astype(BF16)


def permuted(perm, rows):
    return jnp.dot(perm, rows, preferred_element_type=F32).astype(BF16)


def extra_of(terms, ny):
    return ny * -(-terms // ny)


def coef_rows(ref, k, modes, ny):
    return ref.at[k % ny, pl.ds(modes + ny * (k // ny), ny), :]


def turn_kernel(modes, f_ref, a_ref, c_ref, o_ref, e_ref, d_ref, w_ref, *more):
    send, perm = more[:-1], more[-1]
    step = pl.program_id(0)
    chunk, nx, ny, nz = f_ref.shape
    terms = a_ref.shape[0]
    block = block_of(chunk)
    odd = lax.rem(lax.axis_index(GRID), 2)
    outer = ((e_ref, (1 - odd) * (nx - 1)), (d_ref, odd * (nx - 1)))

    @pl.when(step == 0)
    def _():
        perm[...] = one_hot(block, ny)
        for out, x in outer:
            for k in range(terms):
                coef_rows(out, k, modes, ny)[...] = a_ref[k, x]
        arrange(c_ref, w_ref)

    layers = 2 if nx % 2 == 0 else 1
    for x in range(0, nx, layers):
        for q in range(0, chunk, block):
            wide = jnp.concatenate(
                [f_ref[pl.ds(q, block), x + j].reshape(block * ny, nz) for j in range(layers)], axis=1
            )
            wide = permuted(perm[...], wide)
            for j in range(layers):
                o_ref[x + j, :, pl.ds(q, block), :] = wide[:, j * nz:(j + 1) * nz].reshape(ny, block, nz)
    rows = pl.ds(pl.multiple_of(step * chunk, 8), chunk)
    for out, x in outer:
        out[:, rows, :] = o_ref[x]
    for out in send:
        count = out.shape[0]
        out[...] = o_ref[pl.ds((1 - lax.axis_index(MODE)) * (nx - count), count)]


def turn(field, coefs, coupling, sent=0):
    modes, nx, ny, nz = field.shape
    terms, outs, total = coupling.shape
    chunk = divisor(modes, (72, 48, 64, 32, 16, 8))
    outer = (ny, modes + extra_of(coefs.shape[0], ny), nz)
    block = block_of(chunk)
    whole = pl.BlockSpec(outer, lambda i: (0, 0, 0))
    return pl.pallas_call(
        functools.partial(turn_kernel, modes),
        grid=(modes // chunk,),
        in_specs=[
            pl.BlockSpec((chunk, nx, ny, nz), lambda i: (i, 0, 0, 0)),
            pl.BlockSpec(coefs.shape, lambda i: (0, 0, 0, 0)),
            pl.BlockSpec(coupling.shape, lambda i: (0, 0, 0)),
        ],
        out_specs=[pl.BlockSpec((nx, ny, chunk, nz), lambda i: (0, 0, i, 0)), whole, whole]
        + [pl.BlockSpec((outs, terms * total), lambda i: (0, 0))]
        + [pl.BlockSpec((sent, ny, chunk, nz), lambda i: (0, 0, i, 0))] * (sent > 0),
        scratch_shapes=[pltpu.VMEM((block * ny, block * ny), BF16)],
        out_shape=[
            jax.ShapeDtypeStruct((nx, ny, modes, nz), BF16),
            jax.ShapeDtypeStruct(outer, BF16),
            jax.ShapeDtypeStruct(outer, BF16),
            jax.ShapeDtypeStruct((outs, terms * total), BF16),
        ]
        + [jax.ShapeDtypeStruct((sent, ny, modes, nz), BF16)] * (sent > 0),
        compiler_params=grant(field, field, field, field, coefs, coupling, coupling, coupling, coupling),
        name="turn",
    )(field, coefs, coupling)


def chunk_of(total):
    return divisor(total, (32, 16))


def arrange(c_ref, o_ref):
    terms, _, total = c_ref.shape
    chunk = chunk_of(total)
    pieces = [(k, q) for q in range(0, total, chunk) for k in range(terms)]
    per = 128 // chunk
    for i in range(0, len(pieces), per):
        group = pieces[i:i + per]
        wide = jnp.concatenate([c_ref[k, :, q:q + chunk] for k, q in group], axis=1)
        o_ref[:, i * chunk:i * chunk + len(group) * chunk] = wide


class Engine:
    def __init__(self, w_refs, terms, f_ref, stage, coef, face, repx, repy, repz, acc, obuf, perm):
        self.w_refs, self.terms = w_refs, terms
        self.f_ref, self.stage, self.coef, self.face = f_ref, stage, coef, face
        self.repx, self.repy, self.repz = repx, repy, repz
        self.acc, self.obuf, self.perm = acc, obuf, perm
        _, self.ny, self.total, self.nz = stage.shape
        self.outs = acc.shape[1]
        self.block = block_of(self.outs // len(w_refs))

    def prepare(self):
        self.perm[...] = one_hot(self.ny, self.block)
        for slot in range(self.f_ref.shape[0]):
            for y in (0, self.ny + 1):
                self.f_ref[slot, y] = jnp.zeros((self.total, self.nz), F32)

    def spread(self, at, y):
        return jnp.broadcast_to(self.face[at + (pl.ds(y, 1), slice(None))], (16, self.nz)).astype(BF16)

    def faces(self, i, c):
        ny, nz, terms, face = self.ny, self.nz, self.terms, self.face
        lane = lax.broadcasted_iota(jnp.int32, (ny, nz), 1)
        row = lax.broadcasted_iota(jnp.int32, (ny, nz), 0)
        for k in range(terms):
            a = self.coef[c, k]
            face[0, k] = a + self.coef[c - 1, k]
            face[1, k] = a + self.coef[c + 1, k]
            face[2, k] = a + jnp.where(row > 0, pltpu.roll(a, 1, 0), 0.0)
            face[3, k] = a + jnp.where(lane > 0, pltpu.roll(a, 1, 1), 0.0)
            face[4, k] = a + jnp.where(lane < nz - 1, pltpu.roll(a, nz - 1, 1), 0.0)
            face[5, k] = a
        for k in range(terms):
            for y in range(ny):
                self.repx[i, 0, y, k] = self.spread((0, k), y)
                self.repx[i, 1, y, k] = self.spread((1, k), y)
                self.repy[i, y, k] = self.spread((2, k), y)
                self.repz[i, 0, y, k] = self.spread((3, k), y)
                self.repz[i, 1, y, k] = self.spread((4, k), y)
            self.repy[i, ny, k] = self.spread((5, k), ny - 1)

    def widen(self, slot):
        @pl.loop(0, self.ny)
        def _(y):
            self.f_ref[slot, y + 1] = self.stage[slot, y].astype(F32)

    def differences(self, c, y, q):
        lanes = lax.broadcasted_iota(jnp.int32, (16, self.nz), 1)

        def at(c, y):
            return self.f_ref[c, y + 1, pl.ds(q, 16), :]

        def shifted(v, by, edge):
            return jnp.where(lanes != edge, pltpu.roll(v, by, 1), 0.0)

        a, b = at(c, y), at(c, y + 1)
        near = (at(c - 1, y), at(c + 1, y), at(c, y - 1), b, shifted(a, 1, 0), shifted(a, self.nz - 1, self.nz - 1))
        far = (at(c - 1, y + 1), at(c + 1, y + 1), at(c, y + 2), shifted(b, 1, 0), shifted(b, self.nz - 1, self.nz - 1))
        return [(a - v).astype(BF16) for v in near], [(b - v).astype(BF16) for v in far]

    def rows_of(self, i, c, y, q):
        x, yf, z = self.repx, self.repy, self.repz
        both = [self.differences(c, y, q + g) for g in range(0, chunk_of(self.total), 16)]
        sides = ([], [])
        for k in range(self.terms):
            for near, far in both:
                shared = near[3] * yf[i, y + 1, k]
                for j, d, own in ((0, near, near[2] * yf[i, y, k]), (1, far, far[2] * yf[i, y + 2, k])):
                    along_x = d[0] * x[i, 0, y + j, k] + d[1] * x[i, 1, y + j, k]
                    along_y = own + shared if j == 0 else own - shared
                    along_z = d[-2] * z[i, 0, y + j, k] + d[-1] * z[i, 1, y + j, k]
                    sides[j].append(along_x + along_y + along_z)
        return sides

    def pair(self, i, c, n):
        sides = ([], [])
        for q in range(0, self.total, chunk_of(self.total)):
            for side, rows in zip(sides, self.rows_of(i, c, 2 * n, q)):
                side.extend(rows)
        t = jnp.concatenate([jnp.concatenate(side, axis=0) for side in sides], axis=1)
        w = jnp.concatenate([w_ref[...] for w_ref in self.w_refs], axis=0)
        r = jnp.dot(w, t, preferred_element_type=F32).astype(BF16)
        self.acc[2 * n] = r[:, :self.nz]
        self.acc[2 * n + 1] = r[:, self.nz:]

    def layer(self, i, c):
        pairs = self.ny // 2
        unroll = 2 if pairs % 2 == 0 else 1

        @pl.loop(0, pairs // unroll)
        def _(n):
            for j in range(unroll):
                self.pair(i, c, unroll * n + j)

    def finish(self, slot):
        for p in range(0, self.outs, self.block):
            rows = self.acc[:, pl.ds(p, self.block), :].reshape(self.ny * self.block, self.nz)
            rows = permuted(self.perm[...], rows)
            self.obuf[slot, pl.ds(p, self.block)] = rows.reshape(self.block, self.ny, self.nz)


def engine_scratch(slots, items, terms, ny, nz, total, outs, block):
    return [
        pltpu.VMEM((slots, ny + 2, total, nz), F32),
        pltpu.VMEM((slots, ny, total, nz), BF16),
        pltpu.VMEM((slots, terms, ny, nz), F32),
        pltpu.VMEM((6, terms, ny, nz), F32),
        pltpu.VMEM((items, 2, ny, terms, 16, nz), BF16),
        pltpu.VMEM((items, ny + 1, terms, 16, nz), BF16),
        pltpu.VMEM((items, 2, ny, terms, 16, nz), BF16),
        pltpu.VMEM((ny, outs, nz), BF16),
        pltpu.VMEM((2, outs, ny, nz), BF16),
        pltpu.VMEM((block * ny, block * ny), BF16),
    ]


def half_kernel(outer, w_ref, w2_ref, a_ref, own, other, *refs):
    terms, nx, ny, nz = a_ref.shape
    total = w_ref.shape[1] // terms
    modes, outs = total // 2, w_ref.shape[0]
    half = nx // 2
    me = lax.axis_index(MODE)
    if outer:
        halos, refs = refs[:4], refs[5:]
    out_hbm, give_hbm, *refs = refs
    engine = Engine((w_ref, w2_ref), terms, *refs[:10])
    fsem, osem, *more = refs[10:]
    stage, coef = engine.stage, engine.coef
    slots, items = coef.shape[0], engine.repx.shape[0]
    first = me * (half - 1)

    def load(s, slot, ref):
        rows = pl.ds(pl.multiple_of(lax.rem(me + s, 2) * modes, 8), modes)
        return pltpu.make_async_copy(ref, stage.at[slot, :, rows, :], fsem.at[s, slot])

    if outer:
        ends, csem = more
        even, odd = halos[:2], halos[2:]
        takes_odd = (me == 0) == (lax.rem(lax.axis_index(GRID), 2) == 0)
        layer_of = [(1 - me + j, me * (nx - 2) + j) for j in range(2)]
        end = 2 * me
        for test, halo in ((takes_odd, odd), (jnp.logical_not(takes_odd), even)):
            @pl.when(test)
            def _():
                for s in range(2):
                    load(s, end, halo[s].at[:, pl.ds(0, modes), :]).start()
                pltpu.make_async_copy(halo[0].at[:, pl.ds(modes, ends.shape[1]), :], ends, csem).start()
    else:
        layer_of = [(slot, first + slot) for slot in range(slots)]
    for slot, x in layer_of:
        load(0, slot, own.at[x]).start()
        load(1, slot, other.at[x - first]).start()
    engine.prepare()
    for slot, x in layer_of:
        for k in range(terms):
            coef[slot, k] = 0.5 * a_ref[k, x].astype(F32)
    if outer:
        pltpu.make_async_copy(even[0].at[:, pl.ds(modes, ends.shape[1]), :], ends, csem).wait()
        for k in range(terms):
            coef[end, k] = 0.5 * coef_rows(ends, k, 0, ny)[...].astype(F32)

    @pl.loop(0, items)
    def _(i):
        engine.faces(i, i + 1)

    def arrive(slot):
        for s in range(2):
            load(s, slot, own.at[0]).wait()
        engine.widen(slot)

    def writes(i, slot):
        x = me * (nx - 1) if outer else first + i + 1
        return (
            pltpu.make_async_copy(engine.obuf.at[slot, pl.ds(0, outs)], out_hbm.at[:, x], osem.at[0, slot]),
            pltpu.make_async_copy(engine.obuf.at[slot, pl.ds(outs, outs)], give_hbm.at[:, i], osem.at[1, slot]),
        )

    arrive(0)
    arrive(1)

    @pl.loop(0, items)
    def _(i):
        slot = i & 1
        arrive(i + 2)
        engine.layer(i, i + 1)

        @pl.when(i > 1)
        def _():
            for copy in writes(i - 2, slot):
                copy.wait()

        engine.finish(slot)
        for copy in writes(i, slot):
            copy.start()

    for i in range(max(items - 2, 0), items):
        for copy in writes(i, i & 1):
            copy.wait()


def half_layers(weights, coefs, own, other, halos=(), out=()):
    outer = len(halos) > 0
    terms, nx, ny, nz = coefs.shape
    outs, depth = weights[0].shape
    total = depth // terms
    items = 1 if outer else nx // 2 - 1
    slots = items + 2
    block = block_of(outs)
    operands = [*weights, coefs, own, other, *halos, *out]
    scratch = engine_scratch(slots, items, terms, ny, nz, total, 2 * outs, block)
    more = []
    if outer:
        more = [pltpu.VMEM((ny, extra_of(terms, ny), nz), BF16), pltpu.SemaphoreType.DMA]
    return pl.pallas_call(
        functools.partial(half_kernel, outer),
        in_specs=[VMEM, VMEM, VMEM] + [HBM] * (len(operands) - 3),
        out_specs=[HBM, HBM],
        out_shape=[
            jax.ShapeDtypeStruct((outs, nx, ny, nz), BF16),
            jax.ShapeDtypeStruct((outs, items, ny, nz), BF16),
        ],
        input_output_aliases={len(operands) - 1: 0} if outer else {},
        scratch_shapes=[
            *scratch,
            pltpu.SemaphoreType.DMA((2, slots)),
            pltpu.SemaphoreType.DMA((2, 2)),
            *more,
        ],
        compiler_params=grant(*scratch, *weights, coefs),
        cost_estimate=pl.CostEstimate(
            flops=4 * outs * depth * items * ny * nz, bytes_accessed=5 * 2**20, transcendentals=0
        ),
        name="outer" if outer else "inner",
    )(*operands)


def join_kernel(a_ref, b_ref, _, out_hbm, sem):
    nx, inner = out_hbm.shape[1], a_ref.shape[1]
    partner = 1 - lax.axis_index(MODE)
    first = 1 + partner * inner
    copies = [
        pltpu.make_async_copy(a_ref, out_hbm.at[:, pl.ds(first, inner)], sem.at[0]),
        pltpu.make_async_copy(b_ref, out_hbm.at[:, pl.ds(partner * (nx - 1), 1)], sem.at[1]),
    ]
    for copy in copies:
        copy.start()
    for copy in copies:
        copy.wait()


def join(inner, outer, out):
    return pl.pallas_call(
        join_kernel,
        in_specs=[VMEM, VMEM, HBM],
        out_specs=HBM,
        out_shape=jax.ShapeDtypeStruct(out.shape, BF16),
        input_output_aliases={2: 0},
        scratch_shapes=[pltpu.SemaphoreType.DMA((2,))],
        compiler_params=grant(inner, outer),
        name="join",
    )(inner, outer, out)


def layers_kernel(sources, outer, w_ref, a_ref, *refs):
    terms, nx, ny, nz = a_ref.shape
    outs, total = w_ref.shape[0], w_ref.shape[1] // terms
    modes = total // sources
    f_hbm, refs = refs[:sources], refs[sources:]
    if outer:
        even, odd, refs = refs[:sources], refs[sources:2 * sources], refs[2 * sources + 1:]
    out_hbm, *refs = refs
    engine = Engine((w_ref,), terms, *refs[:10])
    fsem, osem, *more = refs[10:]
    stage, coef, obuf = engine.stage, engine.coef, engine.obuf
    slots, items = coef.shape[0], engine.repx.shape[0]
    stride = 3 if outer else 1
    me = lax.axis_index(MODE)
    is_even = lax.rem(lax.axis_index(GRID), 2) == 0

    def place(s):
        return pl.ds(pl.multiple_of(lax.rem(me + s, sources) * modes, 8), modes)

    def load(s, slot, ref):
        return pltpu.make_async_copy(ref, stage.at[slot, :, place(s), :], fsem.at[s, slot])

    layer_of = (None, 0, 1, nx - 2, nx - 1, None) if outer else range(nx)
    if outer:
        ends, csem = more
        copies = []
        for s in range(sources):
            for test, lo, hi in ((is_even, odd[s], even[s]), (~is_even, even[s], odd[s])):
                @pl.when(test)
                def _():
                    load(s, 0, lo.at[:, pl.ds(0, modes), :]).start()
                    load(s, slots - 1, hi.at[:, pl.ds(0, modes), :]).start()
                    if s == 0:
                        for i, ref in ((0, lo), (1, hi)):
                            pltpu.make_async_copy(
                                ref.at[:, pl.ds(modes, ends.shape[2]), :], ends.at[i], csem.at[i]
                            ).start()
    for slot in range(slots):
        if layer_of[slot] is not None:
            for s in range(sources):
                load(s, slot, f_hbm[s].at[layer_of[slot]]).start()

    engine.prepare()
    if outer:
        for i in range(2):
            pltpu.make_async_copy(even[0].at[:, pl.ds(modes, ends.shape[2]), :], ends.at[i], csem.at[i]).wait()
    for slot in range(slots):
        for k in range(terms):
            if layer_of[slot] is None:
                tile = coef_rows(ends.at[0 if slot == 0 else 1], k, 0, ny)[...]
            else:
                tile = a_ref[k, layer_of[slot]]
            coef[slot, k] = 0.5 * tile.astype(F32)

    @pl.loop(0, items)
    def _(i):
        engine.faces(i, 1 + stride * i)

    def arrive(slot):
        for s in range(sources):
            load(s, slot, f_hbm[s].at[0]).wait()
        engine.widen(slot)

    def write(i, slot):
        x = i * (nx - 1) if outer else i + 1
        return pltpu.make_async_copy(obuf.at[slot], out_hbm.at[:, x], osem.at[slot])

    @pl.loop(0, items)
    def _(i):
        slot = i & 1
        if outer:
            for j in range(3):
                arrive(3 * i + j)
        else:
            @pl.when(i == 0)
            def _():
                arrive(0)
                arrive(1)
            arrive(i + 2)

        engine.layer(i, 1 + stride * i)

        @pl.when(i > 1)
        def _():
            write(i - 2, slot).wait()

        engine.finish(slot)
        write(i, slot).start()

    for i in range(max(items - 2, 0), items):
        write(i, i & 1).wait()


def layers(weights, coefs, fields, halos=None, out=None):
    outer = halos is not None
    terms, nx, ny, nz = coefs.shape
    outs, depth = weights.shape
    total = depth // terms
    sources = len(fields)
    block = block_of(outs)
    items = 2 if outer else nx - 2
    slots = 6 if outer else nx
    shape = jax.ShapeDtypeStruct((outs, nx, ny, nz), BF16)
    operands = [weights, coefs, *fields] + ([*halos[0], *halos[1], out] if outer else [])
    scratch = engine_scratch(slots, items, terms, ny, nz, total, outs, block)
    more = []
    if outer:
        more = [pltpu.VMEM((2, ny, extra_of(terms, ny), nz), BF16), pltpu.SemaphoreType.DMA((2,))]
    return pl.pallas_call(
        functools.partial(layers_kernel, sources, outer),
        in_specs=[VMEM, VMEM] + [HBM] * (len(operands) - 2),
        out_specs=HBM,
        out_shape=shape,
        input_output_aliases={len(operands) - 1: 0} if outer else {},
        scratch_shapes=[
            *scratch,
            pltpu.SemaphoreType.DMA((sources, slots)),
            pltpu.SemaphoreType.DMA((2,)),
            *more,
        ],
        compiler_params=grant(*scratch, weights, coefs),
        cost_estimate=pl.CostEstimate(
            flops=2 * outs * depth * items * ny * nz, bytes_accessed=6 * 2**20, transcendentals=0
        ),
        name="outer" if outer else "inner",
    )(*operands)


def solution(mesh):
    sources, bricks = mesh.shape[MODE], mesh.shape[GRID]

    def around(block):
        found = [block]
        for r in range(1, sources):
            found.append(lax.ppermute(block, MODE, [((i + r) % sources, i) for i in range(sources)]))
        return found

    def exchange(block, offset):
        pairs = [(i, i + 1) for i in range(offset, bricks - 1, 2)]
        return lax.ppermute(block, GRID, pairs + [(b, a) for a, b in pairs])

    def halves(field, coupling, coefs):
        def swap(block):
            return lax.ppermute(block, MODE, [(0, 1), (1, 0)])

        turned, even_out, odd_out, weights, send = turn(field, coefs, coupling, coefs.shape[1] // 2 + 1)
        weights = (weights, swap(weights))
        even_in, odd_in = exchange(even_out, 0), exchange(odd_out, 1)
        other = swap(send)
        out, give = half_layers(weights, coefs, turned, other)
        even_in, odd_in, out, give = lax.optimization_barrier((even_in, odd_in, out, give))
        inner = swap(give)
        halos = (even_in, swap(even_in), odd_in, swap(odd_in))
        out, give = half_layers(weights, coefs, turned, other, halos, (out,))
        return join(inner, swap(give), out)

    def body(field, coupling, coefs):
        if sources == 2 and coefs.shape[1] % 2 == 0 and coefs.shape[1] >= 4:
            return halves(field, coupling, coefs)
        turned, even_out, odd_out, weights = turn(field, coefs, coupling)
        even_in, odd_in = exchange(even_out, 0), exchange(odd_out, 1)
        fields = around(turned)
        out = layers(weights, coefs, fields)
        even_in, odd_in, out = lax.optimization_barrier((even_in, odd_in, out))
        return layers(weights, coefs, fields, (around(even_in), around(odd_in)), out)

    spec = P(MODE, GRID, None, None)
    return jax.shard_map(
        body,
        mesh=mesh,
        in_specs=(spec, P(None, MODE, None), P(None, GRID, None, None)),
        out_specs=spec,
        check_vma=False,
    )
```

```python
import functools
import math

import jax
import jax.numpy as jnp
from jax import lax
from jax.experimental import pallas as pl
from jax.experimental.pallas import tpu as pltpu
from jax.sharding import PartitionSpec as P

BF16 = jnp.bfloat16
F32 = jnp.float32
MODE, GRID = "mode", "grid"


def grant(*parts):
    size = sum(math.prod(p.shape) * jnp.dtype(p.dtype).itemsize for p in parts)
    return pltpu.CompilerParams(vmem_limit_bytes=min(size + 10 * 2**20, 60 * 2**20))


VMEM = pl.BlockSpec(memory_space=pltpu.VMEM)
HBM = pl.BlockSpec(memory_space=pl.ANY)


def block_of(rows):
    return 16 if rows % 16 == 0 else 8


def divisor(n, candidates):
    return next(c for c in candidates if n % c == 0)


def one_hot(count, inner):
    size = count * inner
    r = lax.broadcasted_iota(jnp.int32, (size, size), 0)
    c = lax.broadcasted_iota(jnp.int32, (size, size), 1)
    return (c == lax.rem(r, count) * inner + lax.div(r, count)).astype(F32).astype(BF16)


def permuted(perm, rows):
    return jnp.dot(perm, rows, preferred_element_type=F32).astype(BF16)


def extra_of(terms, ny):
    return ny * -(-terms // ny)


def coef_rows(ref, k, modes, ny):
    return ref.at[k % ny, pl.ds(modes + ny * (k // ny), ny), :]


def turn_kernel(chunk, f_hbm, a_hbm, c_hbm, o_ref, e_ref, d_ref, w_ref, *more):
    *send, f_ref, a_ref, c_ref, perm, fsem, sem = more
    modes, nx, ny, nz = f_ref.shape
    terms = a_ref.shape[0]
    block = block_of(chunk)

    def load(q):
        part = pl.ds(q, chunk)
        return pltpu.make_async_copy(f_hbm.at[part], f_ref.at[part], fsem.at[q // chunk])

    others = (
        pltpu.make_async_copy(a_hbm, a_ref, sem.at[0]),
        pltpu.make_async_copy(c_hbm, c_ref, sem.at[1]),
    )
    for q in range(0, modes, chunk):
        load(q).start()
    for copy in others:
        copy.start()
    perm[...] = one_hot(block, ny)
    layers = 2 if nx % 2 == 0 else 1
    for start in range(0, modes, chunk):
        load(start).wait()
        for x in range(0, nx, layers):
            for q in range(start, start + chunk, block):
                wide = jnp.concatenate(
                    [f_ref[pl.ds(q, block), x + j].reshape(block * ny, nz) for j in range(layers)], axis=1
                )
                wide = permuted(perm[...], wide)
                for j in range(layers):
                    o_ref[x + j, :, pl.ds(q, block), :] = wide[:, j * nz:(j + 1) * nz].reshape(ny, block, nz)
    for copy in others:
        copy.wait()
    odd = lax.rem(lax.axis_index(GRID), 2)
    for out, x in ((e_ref, (1 - odd) * (nx - 1)), (d_ref, odd * (nx - 1))):
        out[:, :modes, :] = o_ref[x]
        for k in range(terms):
            coef_rows(out, k, modes, ny)[...] = a_ref[k, x]
    arrange(c_ref, w_ref)
    for out in send:
        count = out.shape[0]
        out[...] = o_ref[pl.ds((1 - lax.axis_index(MODE)) * (nx - count), count)]


def turn(field, coefs, coupling, sent=0):
    modes, nx, ny, nz = field.shape
    terms, outs, total = coupling.shape
    chunk = divisor(modes, (48, 72, 64, 32, 16, 8))
    outer = (ny, modes + extra_of(terms, ny), nz)
    block = block_of(chunk)
    shapes = [(nx, ny, modes, nz), outer, outer, (outs, terms * total)] + [(sent, ny, modes, nz)] * (sent > 0)
    shapes = [jax.ShapeDtypeStruct(shape, BF16) for shape in shapes]
    inputs = [pltpu.with_memory_space_constraint(v, pltpu.HBM) for v in (field, coefs, coupling)]
    return pl.pallas_call(
        functools.partial(turn_kernel, chunk),
        in_specs=[pl.BlockSpec(memory_space=pltpu.HBM)] * 3,
        out_specs=[VMEM] * len(shapes),
        scratch_shapes=[pltpu.VMEM(v.shape, BF16) for v in inputs]
        + [
            pltpu.VMEM((block * ny, block * ny), BF16),
            pltpu.SemaphoreType.DMA((modes // chunk,)),
            pltpu.SemaphoreType.DMA((2,)),
        ],
        out_shape=shapes,
        compiler_params=grant(*inputs, *shapes),
        name="turn",
    )(*inputs)


def chunk_of(total):
    return divisor(total, (32, 16))


def arrange(c_ref, o_ref):
    terms, _, total = c_ref.shape
    chunk = chunk_of(total)
    pieces = [(k, q) for q in range(0, total, chunk) for k in range(terms)]
    per = 128 // chunk
    for i in range(0, len(pieces), per):
        group = pieces[i:i + per]
        wide = jnp.concatenate([c_ref[k, :, q:q + chunk] for k, q in group], axis=1)
        o_ref[:, i * chunk:i * chunk + len(group) * chunk] = wide


class Engine:
    def __init__(self, w_refs, terms, f_ref, coef, face, repx, repy, repz, acc, obuf, perm):
        self.w_refs, self.terms = w_refs, terms
        self.f_ref, self.coef, self.face = f_ref, coef, face
        self.repx, self.repy, self.repz = repx, repy, repz
        self.acc, self.obuf, self.perm = acc, obuf, perm
        _, rows, self.total, self.nz = f_ref.shape
        self.ny = rows - 2
        self.outs = acc.shape[1]
        self.block = block_of(self.outs // len(w_refs))

    def prepare(self):
        self.perm[...] = one_hot(self.ny, self.block)
        for slot in range(self.f_ref.shape[0]):
            for y in (0, self.ny + 1):
                self.f_ref[slot, y] = jnp.zeros((self.total, self.nz), F32)

    def spread(self, at, y):
        return jnp.broadcast_to(self.face[at + (pl.ds(y, 1), slice(None))], (16, self.nz)).astype(BF16)

    def faces(self, i, c):
        ny, nz, terms, face = self.ny, self.nz, self.terms, self.face
        lane = lax.broadcasted_iota(jnp.int32, (ny, nz), 1)
        row = lax.broadcasted_iota(jnp.int32, (ny, nz), 0)
        for k in range(terms):
            a = self.coef[c, k]
            face[0, k] = a + self.coef[c - 1, k]
            face[1, k] = a + self.coef[c + 1, k]
            face[2, k] = a + jnp.where(row > 0, pltpu.roll(a, 1, 0), 0.0)
            face[3, k] = a + jnp.where(lane > 0, pltpu.roll(a, 1, 1), 0.0)
            face[4, k] = a + jnp.where(lane < nz - 1, pltpu.roll(a, nz - 1, 1), 0.0)
            face[5, k] = a
        for k in range(terms):
            for y in range(ny):
                self.repx[i, 0, y, k] = self.spread((0, k), y)
                self.repx[i, 1, y, k] = self.spread((1, k), y)
                self.repy[i, y, k] = self.spread((2, k), y)
                self.repz[i, 0, y, k] = self.spread((3, k), y)
                self.repz[i, 1, y, k] = self.spread((4, k), y)
            self.repy[i, ny, k] = self.spread((5, k), ny - 1)

    def widen(self, slot, parts):
        @pl.loop(0, self.ny)
        def _(y):
            for rows, ref in parts:
                self.f_ref[slot, y + 1, rows, :] = ref[y].astype(F32)

    def differences(self, c, y, q):
        lanes = lax.broadcasted_iota(jnp.int32, (16, self.nz), 1)

        def at(c, y):
            return self.f_ref[c, y + 1, pl.ds(q, 16), :]

        def shifted(v, by, edge):
            return jnp.where(lanes != edge, pltpu.roll(v, by, 1), 0.0)

        a, b = at(c, y), at(c, y + 1)
        near = (at(c - 1, y), at(c + 1, y), at(c, y - 1), b, shifted(a, 1, 0), shifted(a, self.nz - 1, self.nz - 1))
        far = (at(c - 1, y + 1), at(c + 1, y + 1), at(c, y + 2), shifted(b, 1, 0), shifted(b, self.nz - 1, self.nz - 1))
        return [(a - v).astype(BF16) for v in near], [(b - v).astype(BF16) for v in far]

    def rows_of(self, i, c, y, q):
        x, yf, z = self.repx, self.repy, self.repz
        both = [self.differences(c, y, q + g) for g in range(0, chunk_of(self.total), 16)]
        sides = ([], [])
        for k in range(self.terms):
            for near, far in both:
                shared = near[3] * yf[i, y + 1, k]
                for j, d, own in ((0, near, near[2] * yf[i, y, k]), (1, far, far[2] * yf[i, y + 2, k])):
                    along_x = d[0] * x[i, 0, y + j, k] + d[1] * x[i, 1, y + j, k]
                    along_y = own + shared if j == 0 else own - shared
                    along_z = d[-2] * z[i, 0, y + j, k] + d[-1] * z[i, 1, y + j, k]
                    sides[j].append(along_x + along_y + along_z)
        return sides

    def pair(self, i, c, n):
        sides = ([], [])
        for q in range(0, self.total, chunk_of(self.total)):
            for side, rows in zip(sides, self.rows_of(i, c, 2 * n, q)):
                side.extend(rows)
        t = jnp.concatenate([jnp.concatenate(side, axis=0) for side in sides], axis=1)
        w = jnp.concatenate([w_ref[...] for w_ref in self.w_refs], axis=0)
        r = jnp.dot(w, t, preferred_element_type=F32).astype(BF16)
        self.acc[2 * n] = r[:, :self.nz]
        self.acc[2 * n + 1] = r[:, self.nz:]

    def layer(self, i, c):
        pairs = self.ny // 2
        unroll = divisor(pairs, (4, 2, 1))

        @pl.loop(0, pairs // unroll)
        def _(n):
            for j in range(unroll):
                self.pair(i, c, unroll * n + j)

    def finish(self, slot):
        for p in range(0, self.outs, self.block):
            rows = self.acc[:, pl.ds(p, self.block), :].reshape(self.ny * self.block, self.nz)
            rows = permuted(self.perm[...], rows)
            self.obuf[slot, pl.ds(p, self.block)] = rows.reshape(self.block, self.ny, self.nz)


def engine_scratch(slots, items, terms, ny, nz, total, outs, block):
    return [
        pltpu.VMEM((slots, ny + 2, total, nz), F32),
        pltpu.VMEM((slots, terms, ny, nz), F32),
        pltpu.VMEM((6, terms, ny, nz), F32),
        pltpu.VMEM((items, 2, ny, terms, 16, nz), BF16),
        pltpu.VMEM((items, ny + 1, terms, 16, nz), BF16),
        pltpu.VMEM((items, 2, ny, terms, 16, nz), BF16),
        pltpu.VMEM((ny, outs, nz), BF16),
        pltpu.VMEM((2, outs, ny, nz), BF16),
        pltpu.VMEM((block * ny, block * ny), BF16),
    ]


def half_kernel(outer, w_ref, w2_ref, a_ref, own, other, *refs):
    terms, nx, ny, nz = a_ref.shape
    total = w_ref.shape[1] // terms
    modes, outs = total // 2, w_ref.shape[0]
    half = nx // 2
    me = lax.axis_index(MODE)
    if outer:
        halos, refs = refs[:4], refs[5:]
    out_hbm, give_hbm, *refs = refs
    engine = Engine((w_ref, w2_ref), terms, *refs[:9])
    osem = refs[9]
    coef = engine.coef
    slots, items = coef.shape[0], engine.repx.shape[0]
    first = me * (half - 1)
    aligned = 16 if modes % 16 == 0 else 8
    places = [pl.ds(pl.multiple_of(lax.rem(me + s, 2) * modes, aligned), modes) for s in range(2)]
    engine.prepare()
    if outer:
        even, odd = halos[:2], halos[2:]
        takes_odd = (me == 0) == (lax.rem(lax.axis_index(GRID), 2) == 0)
        layer_of = [(1 - me + j, me * (nx - 2) + j) for j in range(2)]
        end = 2 * me
        for test, halo in ((takes_odd, odd), (jnp.logical_not(takes_odd), even)):
            @pl.when(test)
            def _():
                engine.widen(end, [(rows, ref.at[:, :modes, :]) for rows, ref in zip(places, halo)])
                for k in range(terms):
                    coef[end, k] = 0.5 * coef_rows(halo[0], k, modes, ny)[...].astype(F32)
    else:
        layer_of = [(slot, first + slot) for slot in range(slots)]
    for slot, x in layer_of:
        engine.widen(slot, ((places[0], own.at[x]), (places[1], other.at[x - first])))
        for k in range(terms):
            coef[slot, k] = 0.5 * a_ref[k, x].astype(F32)

    @pl.loop(0, items)
    def _(i):
        engine.faces(i, i + 1)

    def writes(i, slot):
        x = me * (nx - 1) if outer else first + i + 1
        return (
            pltpu.make_async_copy(engine.obuf.at[slot, pl.ds(0, outs)], out_hbm.at[:, x], osem.at[0, slot]),
            pltpu.make_async_copy(engine.obuf.at[slot, pl.ds(outs, outs)], give_hbm.at[:, i], osem.at[1, slot]),
        )

    @pl.loop(0, items)
    def _(i):
        slot = i & 1
        engine.layer(i, i + 1)

        @pl.when(i > 1)
        def _():
            for copy in writes(i - 2, slot):
                copy.wait()

        engine.finish(slot)
        for copy in writes(i, slot):
            copy.start()

    for i in range(max(items - 2, 0), items):
        for copy in writes(i, i & 1):
            copy.wait()


def half_layers(weights, coefs, own, other, halos=(), out=()):
    outer = len(halos) > 0
    terms, nx, ny, nz = coefs.shape
    outs, depth = weights[0].shape
    total = depth // terms
    items = 1 if outer else nx // 2 - 1
    slots = items + 2
    block = block_of(outs)
    operands = [*weights, coefs, own, other, *halos, *out]
    scratch = engine_scratch(slots, items, terms, ny, nz, total, 2 * outs, block)
    return pl.pallas_call(
        functools.partial(half_kernel, outer),
        in_specs=[VMEM] * (5 + len(halos)) + [HBM] * len(out),
        out_specs=[HBM, HBM],
        out_shape=[
            jax.ShapeDtypeStruct((outs, nx, ny, nz), BF16),
            jax.ShapeDtypeStruct((outs, items, ny, nz), BF16),
        ],
        input_output_aliases={len(operands) - 1: 0} if outer else {},
        scratch_shapes=[
            *scratch,
            pltpu.SemaphoreType.DMA((2, 2)),
        ],
        compiler_params=grant(*scratch),
        cost_estimate=pl.CostEstimate(
            flops=4 * outs * depth * items * ny * nz, bytes_accessed=5 * 2**20, transcendentals=0
        ),
        name="outer" if outer else "inner",
    )(*operands)


def join_kernel(a_ref, b_ref, _, out_hbm, sem):
    nx, inner = out_hbm.shape[1], a_ref.shape[1]
    partner = 1 - lax.axis_index(MODE)
    first = 1 + partner * inner
    copies = [
        pltpu.make_async_copy(a_ref, out_hbm.at[:, pl.ds(first, inner)], sem.at[0]),
        pltpu.make_async_copy(b_ref, out_hbm.at[:, pl.ds(partner * (nx - 1), 1)], sem.at[1]),
    ]
    for copy in copies:
        copy.start()
    for copy in copies:
        copy.wait()


def join(inner, outer, out):
    return pl.pallas_call(
        join_kernel,
        in_specs=[VMEM, VMEM, HBM],
        out_specs=HBM,
        out_shape=jax.ShapeDtypeStruct(out.shape, BF16),
        input_output_aliases={2: 0},
        scratch_shapes=[pltpu.SemaphoreType.DMA((2,))],
        compiler_params=grant(inner, outer),
        name="join",
    )(inner, outer, out)


def layers_kernel(sources, outer, w_ref, a_ref, *refs):
    terms, nx, ny, nz = a_ref.shape
    outs, total = w_ref.shape[0], w_ref.shape[1] // terms
    modes = total // sources
    f_hbm, refs = refs[:sources], refs[sources:]
    if outer:
        even, odd, refs = refs[:sources], refs[sources:2 * sources], refs[2 * sources + 1:]
    out_hbm, *refs = refs
    engine = Engine((w_ref,), terms, *refs[:9])
    stage, fsem, osem, *more = refs[9:]
    coef, obuf = engine.coef, engine.obuf
    slots, items = coef.shape[0], engine.repx.shape[0]
    stride = 3 if outer else 1
    me = lax.axis_index(MODE)
    is_even = lax.rem(lax.axis_index(GRID), 2) == 0

    def place(s):
        return pl.ds(pl.multiple_of(lax.rem(me + s, sources) * modes, 8), modes)

    def load(s, slot, ref):
        return pltpu.make_async_copy(ref, stage.at[slot, :, place(s), :], fsem.at[s, slot])

    layer_of = (None, 0, 1, nx - 2, nx - 1, None) if outer else range(nx)
    if outer:
        ends, csem = more
        copies = []
        for s in range(sources):
            for test, lo, hi in ((is_even, odd[s], even[s]), (~is_even, even[s], odd[s])):
                @pl.when(test)
                def _():
                    load(s, 0, lo.at[:, pl.ds(0, modes), :]).start()
                    load(s, slots - 1, hi.at[:, pl.ds(0, modes), :]).start()
                    if s == 0:
                        for i, ref in ((0, lo), (1, hi)):
                            pltpu.make_async_copy(
                                ref.at[:, pl.ds(modes, ends.shape[2]), :], ends.at[i], csem.at[i]
                            ).start()
    for slot in range(slots):
        if layer_of[slot] is not None:
            for s in range(sources):
                load(s, slot, f_hbm[s].at[layer_of[slot]]).start()

    engine.prepare()
    if outer:
        for i in range(2):
            pltpu.make_async_copy(even[0].at[:, pl.ds(modes, ends.shape[2]), :], ends.at[i], csem.at[i]).wait()
    for slot in range(slots):
        for k in range(terms):
            if layer_of[slot] is None:
                tile = coef_rows(ends.at[0 if slot == 0 else 1], k, 0, ny)[...]
            else:
                tile = a_ref[k, layer_of[slot]]
            coef[slot, k] = 0.5 * tile.astype(F32)

    @pl.loop(0, items)
    def _(i):
        engine.faces(i, 1 + stride * i)

    def arrive(slot):
        for s in range(sources):
            load(s, slot, f_hbm[s].at[0]).wait()
        engine.widen(slot, ((slice(None), stage.at[slot]),))

    def write(i, slot):
        x = i * (nx - 1) if outer else i + 1
        return pltpu.make_async_copy(obuf.at[slot], out_hbm.at[:, x], osem.at[slot])

    @pl.loop(0, items)
    def _(i):
        slot = i & 1
        if outer:
            for j in range(3):
                arrive(3 * i + j)
        else:
            @pl.when(i == 0)
            def _():
                arrive(0)
                arrive(1)
            arrive(i + 2)

        engine.layer(i, 1 + stride * i)

        @pl.when(i > 1)
        def _():
            write(i - 2, slot).wait()

        engine.finish(slot)
        write(i, slot).start()

    for i in range(max(items - 2, 0), items):
        write(i, i & 1).wait()


def layers(weights, coefs, fields, halos=None, out=None):
    outer = halos is not None
    terms, nx, ny, nz = coefs.shape
    outs, depth = weights.shape
    total = depth // terms
    sources = len(fields)
    block = block_of(outs)
    items = 2 if outer else nx - 2
    slots = 6 if outer else nx
    shape = jax.ShapeDtypeStruct((outs, nx, ny, nz), BF16)
    operands = [weights, coefs, *fields] + ([*halos[0], *halos[1], out] if outer else [])
    scratch = engine_scratch(slots, items, terms, ny, nz, total, outs, block)
    scratch.append(pltpu.VMEM((slots, ny, total, nz), BF16))
    more = []
    if outer:
        more = [pltpu.VMEM((2, ny, extra_of(terms, ny), nz), BF16), pltpu.SemaphoreType.DMA((2,))]
    return pl.pallas_call(
        functools.partial(layers_kernel, sources, outer),
        in_specs=[VMEM, VMEM] + [HBM] * (len(operands) - 2),
        out_specs=HBM,
        out_shape=shape,
        input_output_aliases={len(operands) - 1: 0} if outer else {},
        scratch_shapes=[
            *scratch,
            pltpu.SemaphoreType.DMA((sources, slots)),
            pltpu.SemaphoreType.DMA((2,)),
            *more,
        ],
        compiler_params=grant(*scratch, weights, coefs),
        cost_estimate=pl.CostEstimate(
            flops=2 * outs * depth * items * ny * nz, bytes_accessed=6 * 2**20, transcendentals=0
        ),
        name="outer" if outer else "inner",
    )(*operands)


def solution(mesh):
    sources, bricks = mesh.shape[MODE], mesh.shape[GRID]

    def around(block):
        found = [block]
        for r in range(1, sources):
            found.append(lax.ppermute(block, MODE, [((i + r) % sources, i) for i in range(sources)]))
        return found

    def exchange(block, offset):
        pairs = [(i, i + 1) for i in range(offset, bricks - 1, 2)]
        return lax.ppermute(block, GRID, pairs + [(b, a) for a, b in pairs])

    def halves(field, coupling, coefs):
        def swap(block):
            return lax.ppermute(block, MODE, [(0, 1), (1, 0)])

        turned, even_out, odd_out, weights, send = turn(field, coefs, coupling, coefs.shape[1] // 2 + 1)
        weights = (weights, swap(weights))
        even_in, odd_in = exchange(even_out, 0), exchange(odd_out, 1)
        other = swap(send)
        out, give = half_layers(weights, coefs, turned, other)
        even_in, odd_in, out, give = lax.optimization_barrier((even_in, odd_in, out, give))
        inner = swap(give)
        halos = (even_in, swap(even_in), odd_in, swap(odd_in))
        out, give = half_layers(weights, coefs, turned, other, halos, (out,))
        return join(inner, swap(give), out)

    def body(field, coupling, coefs):
        if sources == 2 and coefs.shape[1] % 2 == 0 and coefs.shape[1] >= 4:
            return halves(field, coupling, coefs)
        turned, even_out, odd_out, weights = turn(field, coefs, coupling)
        even_in, odd_in = exchange(even_out, 0), exchange(odd_out, 1)
        fields = around(turned)
        out = layers(weights, coefs, fields)
        even_in, odd_in, out = lax.optimization_barrier((even_in, odd_in, out))
        return layers(weights, coefs, fields, (around(even_in), around(odd_in)), out)

    spec = P(MODE, GRID, None, None)
    return jax.shard_map(
        body,
        mesh=mesh,
        in_specs=(spec, P(None, MODE, None), P(None, GRID, None, None)),
        out_specs=spec,
        check_vma=False,
    )
```

```python
import functools
import math

import jax
import jax.numpy as jnp
from jax import lax
from jax.experimental import pallas as pl
from jax.experimental.pallas import tpu as pltpu
from jax.sharding import PartitionSpec as P

BF16 = jnp.bfloat16
F32 = jnp.float32
MODE, GRID = "mode", "grid"


def grant(*parts):
    size = sum(math.prod(p.shape) * jnp.dtype(p.dtype).itemsize for p in parts)
    return pltpu.CompilerParams(vmem_limit_bytes=min(size + 10 * 2**20, 60 * 2**20))


VMEM = pl.BlockSpec(memory_space=pltpu.VMEM)
HBM = pl.BlockSpec(memory_space=pl.ANY)


def block_of(rows):
    return 16 if rows % 16 == 0 else 8


def divisor(n, candidates):
    return next(c for c in candidates if n % c == 0)


def one_hot(count, inner):
    size = count * inner
    r = lax.broadcasted_iota(jnp.int32, (size, size), 0)
    c = lax.broadcasted_iota(jnp.int32, (size, size), 1)
    return (c == lax.rem(r, count) * inner + lax.div(r, count)).astype(F32).astype(BF16)


def permuted(perm, rows):
    return jnp.dot(perm, rows, preferred_element_type=F32).astype(BF16)


def extra_of(terms, ny):
    return ny * -(-terms // ny)


def coef_rows(ref, k, modes, ny):
    return ref.at[k % ny, pl.ds(modes + ny * (k // ny), ny), :]


def turn_kernel(chunk, f_hbm, a_hbm, c_hbm, o_ref, e_ref, d_ref, w_ref, *more):
    *send, f_ref, a_ref, c_ref, perm, fsem, sem = more
    modes, nx, ny, nz = f_ref.shape
    terms = a_ref.shape[0]
    block = block_of(chunk)

    def load(q):
        part = pl.ds(q, chunk)
        return pltpu.make_async_copy(f_hbm.at[part], f_ref.at[part], fsem.at[q // chunk])

    others = (
        pltpu.make_async_copy(a_hbm, a_ref, sem.at[0]),
        pltpu.make_async_copy(c_hbm, c_ref, sem.at[1]),
    )
    for q in range(0, modes, chunk):
        load(q).start()
    for copy in others:
        copy.start()
    perm[...] = one_hot(block, ny)
    layers = 2 if nx % 2 == 0 else 1
    for start in range(0, modes, chunk):
        load(start).wait()
        for x in range(0, nx, layers):
            for q in range(start, start + chunk, block):
                wide = jnp.concatenate(
                    [f_ref[pl.ds(q, block), x + j].reshape(block * ny, nz) for j in range(layers)], axis=1
                )
                wide = permuted(perm[...], wide)
                for j in range(layers):
                    o_ref[x + j, :, pl.ds(q, block), :] = wide[:, j * nz:(j + 1) * nz].reshape(ny, block, nz)
    for copy in others:
        copy.wait()
    odd = lax.rem(lax.axis_index(GRID), 2)
    for out, x in ((e_ref, (1 - odd) * (nx - 1)), (d_ref, odd * (nx - 1))):
        out[:, :modes, :] = o_ref[x]
        if send:
            for k in range(terms):
                @pl.when(k // ny % 2 == lax.axis_index(MODE))
                def _():
                    coef_rows(out, k // (2 * ny) * ny + k % ny, modes, ny)[...] = a_ref[k, x]
        else:
            for k in range(terms):
                coef_rows(out, k, modes, ny)[...] = a_ref[k, x]
    arrange(c_ref, w_ref)
    for out in send:
        count = out.shape[0]
        out[...] = o_ref[pl.ds((1 - lax.axis_index(MODE)) * (nx - count), count)]


def turn(field, coefs, coupling, sent=0):
    modes, nx, ny, nz = field.shape
    terms, outs, total = coupling.shape
    chunk = divisor(modes, (48, 72, 64, 32, 16, 8))
    outer = (ny, modes + extra_of(-(-terms // 2) if sent else terms, ny), nz)
    block = block_of(chunk)
    shapes = [(nx, ny, modes, nz), outer, outer, (outs, terms * total)] + [(sent, ny, modes, nz)] * (sent > 0)
    shapes = [jax.ShapeDtypeStruct(shape, BF16) for shape in shapes]
    inputs = [pltpu.with_memory_space_constraint(v, pltpu.HBM) for v in (field, coefs, coupling)]
    return pl.pallas_call(
        functools.partial(turn_kernel, chunk),
        in_specs=[pl.BlockSpec(memory_space=pltpu.HBM)] * 3,
        out_specs=[VMEM] * len(shapes),
        scratch_shapes=[pltpu.VMEM(v.shape, BF16) for v in inputs]
        + [
            pltpu.VMEM((block * ny, block * ny), BF16),
            pltpu.SemaphoreType.DMA((modes // chunk,)),
            pltpu.SemaphoreType.DMA((2,)),
        ],
        out_shape=shapes,
        compiler_params=grant(*inputs, *shapes),
        name="turn",
    )(*inputs)


def chunk_of(total):
    return divisor(total, (32, 16))


def arrange(c_ref, o_ref):
    terms, _, total = c_ref.shape
    chunk = chunk_of(total)
    pieces = [(k, q) for q in range(0, total, chunk) for k in range(terms)]
    per = 128 // chunk
    for i in range(0, len(pieces), per):
        group = pieces[i:i + per]
        wide = jnp.concatenate([c_ref[k, :, q:q + chunk] for k, q in group], axis=1)
        o_ref[:, i * chunk:i * chunk + len(group) * chunk] = wide


class Engine:
    def __init__(self, w_refs, terms, f_ref, coef, face, repx, repy, repz, acc, obuf, perm):
        self.w_refs, self.terms = w_refs, terms
        self.f_ref, self.coef, self.face = f_ref, coef, face
        self.repx, self.repy, self.repz = repx, repy, repz
        self.acc, self.obuf, self.perm = acc, obuf, perm
        _, rows, self.total, self.nz = f_ref.shape
        self.ny = rows - 2
        self.outs = acc.shape[1]
        self.block = block_of(self.outs // len(w_refs))

    def prepare(self):
        self.perm[...] = one_hot(self.ny, self.block)
        for slot in range(self.f_ref.shape[0]):
            for y in (0, self.ny + 1):
                self.f_ref[slot, y] = jnp.zeros((self.total, self.nz), F32)

    def spread(self, at, y):
        return jnp.broadcast_to(self.face[at + (pl.ds(y, 1), slice(None))], (16, self.nz)).astype(BF16)

    def faces(self, i, c):
        ny, nz, terms, face = self.ny, self.nz, self.terms, self.face
        lane = lax.broadcasted_iota(jnp.int32, (ny, nz), 1)
        row = lax.broadcasted_iota(jnp.int32, (ny, nz), 0)
        for k in range(terms):
            a = self.coef[c, k]
            face[0, k] = a + self.coef[c - 1, k]
            face[1, k] = a + self.coef[c + 1, k]
            face[2, k] = a + jnp.where(row > 0, pltpu.roll(a, 1, 0), 0.0)
            face[3, k] = a + jnp.where(lane > 0, pltpu.roll(a, 1, 1), 0.0)
            face[4, k] = a + jnp.where(lane < nz - 1, pltpu.roll(a, nz - 1, 1), 0.0)
            face[5, k] = a
        for k in range(terms):
            for y in range(ny):
                self.repx[i, 0, y, k] = self.spread((0, k), y)
                self.repx[i, 1, y, k] = self.spread((1, k), y)
                self.repy[i, y, k] = self.spread((2, k), y)
                self.repz[i, 0, y, k] = self.spread((3, k), y)
                self.repz[i, 1, y, k] = self.spread((4, k), y)
            self.repy[i, ny, k] = self.spread((5, k), ny - 1)

    def widen(self, slot, parts):
        @pl.loop(0, self.ny)
        def _(y):
            for rows, ref in parts:
                self.f_ref[slot, y + 1, rows, :] = ref[y].astype(F32)

    def differences(self, c, y, q):
        lanes = lax.broadcasted_iota(jnp.int32, (16, self.nz), 1)

        def at(c, y):
            return self.f_ref[c, y + 1, pl.ds(q, 16), :]

        def shifted(v, by, edge):
            return jnp.where(lanes != edge, pltpu.roll(v, by, 1), 0.0)

        a, b = at(c, y), at(c, y + 1)
        near = (at(c - 1, y), at(c + 1, y), at(c, y - 1), b, shifted(a, 1, 0), shifted(a, self.nz - 1, self.nz - 1))
        far = (at(c - 1, y + 1), at(c + 1, y + 1), at(c, y + 2), shifted(b, 1, 0), shifted(b, self.nz - 1, self.nz - 1))
        return [(a - v).astype(BF16) for v in near], [(b - v).astype(BF16) for v in far]

    def rows_of(self, i, c, y, q):
        x, yf, z = self.repx, self.repy, self.repz
        both = [self.differences(c, y, q + g) for g in range(0, chunk_of(self.total), 16)]
        sides = ([], [])
        for k in range(self.terms):
            for near, far in both:
                shared = near[3] * yf[i, y + 1, k]
                for j, d, own in ((0, near, near[2] * yf[i, y, k]), (1, far, far[2] * yf[i, y + 2, k])):
                    along_x = d[0] * x[i, 0, y + j, k] + d[1] * x[i, 1, y + j, k]
                    along_y = own + shared if j == 0 else own - shared
                    along_z = d[-2] * z[i, 0, y + j, k] + d[-1] * z[i, 1, y + j, k]
                    sides[j].append(along_x + along_y + along_z)
        return sides

    def pair(self, i, c, n):
        sides = ([], [])
        for q in range(0, self.total, chunk_of(self.total)):
            for side, rows in zip(sides, self.rows_of(i, c, 2 * n, q)):
                side.extend(rows)
        t = jnp.concatenate([jnp.concatenate(side, axis=0) for side in sides], axis=1)
        w = jnp.concatenate([w_ref[...] for w_ref in self.w_refs], axis=0)
        r = jnp.dot(w, t, preferred_element_type=F32).astype(BF16)
        self.acc[2 * n] = r[:, :self.nz]
        self.acc[2 * n + 1] = r[:, self.nz:]

    def layer(self, i, c):
        pairs = self.ny // 2
        unroll = divisor(pairs, (4, 2, 1))

        @pl.loop(0, pairs // unroll)
        def _(n):
            for j in range(unroll):
                self.pair(i, c, unroll * n + j)

    def finish(self, slot):
        for p in range(0, self.outs, self.block):
            rows = self.acc[:, pl.ds(p, self.block), :].reshape(self.ny * self.block, self.nz)
            rows = permuted(self.perm[...], rows)
            self.obuf[slot, pl.ds(p, self.block)] = rows.reshape(self.block, self.ny, self.nz)


def engine_scratch(slots, items, terms, ny, nz, total, outs, block):
    return [
        pltpu.VMEM((slots, ny + 2, total, nz), F32),
        pltpu.VMEM((slots, terms, ny, nz), F32),
        pltpu.VMEM((6, terms, ny, nz), F32),
        pltpu.VMEM((items, 2, ny, terms, 16, nz), BF16),
        pltpu.VMEM((items, ny + 1, terms, 16, nz), BF16),
        pltpu.VMEM((items, 2, ny, terms, 16, nz), BF16),
        pltpu.VMEM((ny, outs, nz), BF16),
        pltpu.VMEM((2, outs, ny, nz), BF16),
        pltpu.VMEM((block * ny, block * ny), BF16),
    ]


def half_kernel(outer, w_ref, w2_ref, a_ref, own, other, *refs):
    terms, nx, ny, nz = a_ref.shape
    total = w_ref.shape[1] // terms
    modes, outs = total // 2, w_ref.shape[0]
    half = nx // 2
    me = lax.axis_index(MODE)
    if outer:
        halos, refs = refs[:4], refs[5:]
    out_hbm, give_hbm, *refs = refs
    engine = Engine((w_ref, w2_ref), terms, *refs[:9])
    osem = refs[9]
    coef = engine.coef
    slots, items = coef.shape[0], engine.repx.shape[0]
    first = me * (half - 1)
    aligned = 16 if modes % 16 == 0 else 8
    places = [pl.ds(pl.multiple_of(lax.rem(me + s, 2) * modes, aligned), modes) for s in range(2)]
    engine.prepare()
    if outer:
        even, odd = halos[:2], halos[2:]
        takes_odd = (me == 0) == (lax.rem(lax.axis_index(GRID), 2) == 0)
        layer_of = [(1 - me + j, me * (nx - 2) + j) for j in range(2)]
        end = 2 * me
        for test, halo in ((takes_odd, odd), (jnp.logical_not(takes_odd), even)):
            @pl.when(test)
            def _():
                engine.widen(end, [(rows, ref.at[:, :modes, :]) for rows, ref in zip(places, halo)])
                for k in range(terms):
                    tiles = [coef_rows(ref, k // (2 * ny) * ny + k % ny, modes, ny)[...].astype(F32) for ref in halo]
                    coef[end, k] = 0.5 * jnp.where(k // ny % 2 == me, tiles[0], tiles[1])
    else:
        layer_of = [(slot, first + slot) for slot in range(slots)]
    for slot, x in layer_of:
        engine.widen(slot, ((places[0], own.at[x]), (places[1], other.at[x - first])))
        for k in range(terms):
            coef[slot, k] = 0.5 * a_ref[k, x].astype(F32)

    @pl.loop(0, items)
    def _(i):
        engine.faces(i, i + 1)

    def writes(i, slot):
        x = me * (nx - 1) if outer else first + i + 1
        return (
            pltpu.make_async_copy(engine.obuf.at[slot, pl.ds(0, outs)], out_hbm.at[:, x], osem.at[0, slot]),
            pltpu.make_async_copy(engine.obuf.at[slot, pl.ds(outs, outs)], give_hbm.at[:, i], osem.at[1, slot]),
        )

    @pl.loop(0, items)
    def _(i):
        slot = i & 1
        engine.layer(i, i + 1)

        @pl.when(i > 1)
        def _():
            for copy in writes(i - 2, slot):
                copy.wait()

        engine.finish(slot)
        for copy in writes(i, slot):
            copy.start()

    for i in range(max(items - 2, 0), items):
        for copy in writes(i, i & 1):
            copy.wait()


def half_layers(weights, coefs, own, other, halos=(), out=()):
    outer = len(halos) > 0
    terms, nx, ny, nz = coefs.shape
    outs, depth = weights[0].shape
    total = depth // terms
    items = 1 if outer else nx // 2 - 1
    slots = items + 2
    block = block_of(outs)
    operands = [*weights, coefs, own, other, *halos, *out]
    scratch = engine_scratch(slots, items, terms, ny, nz, total, 2 * outs, block)
    return pl.pallas_call(
        functools.partial(half_kernel, outer),
        in_specs=[VMEM] * (5 + len(halos)) + [HBM] * len(out),
        out_specs=[HBM, HBM],
        out_shape=[
            jax.ShapeDtypeStruct((outs, nx, ny, nz), BF16),
            jax.ShapeDtypeStruct((outs, items, ny, nz), BF16),
        ],
        input_output_aliases={len(operands) - 1: 0} if outer else {},
        scratch_shapes=[
            *scratch,
            pltpu.SemaphoreType.DMA((2, 2)),
        ],
        compiler_params=grant(*scratch),
        cost_estimate=pl.CostEstimate(
            flops=4 * outs * depth * items * ny * nz, bytes_accessed=5 * 2**20, transcendentals=0
        ),
        name="outer" if outer else "inner",
    )(*operands)


def join_kernel(a_ref, b_ref, _, out_hbm, sem):
    nx, inner = out_hbm.shape[1], a_ref.shape[1]
    partner = 1 - lax.axis_index(MODE)
    first = 1 + partner * inner
    copies = [
        pltpu.make_async_copy(a_ref, out_hbm.at[:, pl.ds(first, inner)], sem.at[0]),
        pltpu.make_async_copy(b_ref, out_hbm.at[:, pl.ds(partner * (nx - 1), 1)], sem.at[1]),
    ]
    for copy in copies:
        copy.start()
    for copy in copies:
        copy.wait()


def join(inner, outer, out):
    return pl.pallas_call(
        join_kernel,
        in_specs=[VMEM, VMEM, HBM],
        out_specs=HBM,
        out_shape=jax.ShapeDtypeStruct(out.shape, BF16),
        input_output_aliases={2: 0},
        scratch_shapes=[pltpu.SemaphoreType.DMA((2,))],
        compiler_params=grant(inner, outer),
        name="join",
    )(inner, outer, out)


def layers_kernel(sources, outer, w_ref, a_ref, *refs):
    terms, nx, ny, nz = a_ref.shape
    outs, total = w_ref.shape[0], w_ref.shape[1] // terms
    modes = total // sources
    f_hbm, refs = refs[:sources], refs[sources:]
    if outer:
        even, odd, refs = refs[:sources], refs[sources:2 * sources], refs[2 * sources + 1:]
    out_hbm, *refs = refs
    engine = Engine((w_ref,), terms, *refs[:9])
    stage, fsem, osem, *more = refs[9:]
    coef, obuf = engine.coef, engine.obuf
    slots, items = coef.shape[0], engine.repx.shape[0]
    stride = 3 if outer else 1
    me = lax.axis_index(MODE)
    is_even = lax.rem(lax.axis_index(GRID), 2) == 0

    def place(s):
        return pl.ds(pl.multiple_of(lax.rem(me + s, sources) * modes, 8), modes)

    def load(s, slot, ref):
        return pltpu.make_async_copy(ref, stage.at[slot, :, place(s), :], fsem.at[s, slot])

    layer_of = (None, 0, 1, nx - 2, nx - 1, None) if outer else range(nx)
    if outer:
        ends, csem = more
        copies = []
        for s in range(sources):
            for test, lo, hi in ((is_even, odd[s], even[s]), (~is_even, even[s], odd[s])):
                @pl.when(test)
                def _():
                    load(s, 0, lo.at[:, pl.ds(0, modes), :]).start()
                    load(s, slots - 1, hi.at[:, pl.ds(0, modes), :]).start()
                    if s == 0:
                        for i, ref in ((0, lo), (1, hi)):
                            pltpu.make_async_copy(
                                ref.at[:, pl.ds(modes, ends.shape[2]), :], ends.at[i], csem.at[i]
                            ).start()
    for slot in range(slots):
        if layer_of[slot] is not None:
            for s in range(sources):
                load(s, slot, f_hbm[s].at[layer_of[slot]]).start()

    engine.prepare()
    if outer:
        for i in range(2):
            pltpu.make_async_copy(even[0].at[:, pl.ds(modes, ends.shape[2]), :], ends.at[i], csem.at[i]).wait()
    for slot in range(slots):
        for k in range(terms):
            if layer_of[slot] is None:
                tile = coef_rows(ends.at[0 if slot == 0 else 1], k, 0, ny)[...]
            else:
                tile = a_ref[k, layer_of[slot]]
            coef[slot, k] = 0.5 * tile.astype(F32)

    @pl.loop(0, items)
    def _(i):
        engine.faces(i, 1 + stride * i)

    def arrive(slot):
        for s in range(sources):
            load(s, slot, f_hbm[s].at[0]).wait()
        engine.widen(slot, ((slice(None), stage.at[slot]),))

    def write(i, slot):
        x = i * (nx - 1) if outer else i + 1
        return pltpu.make_async_copy(obuf.at[slot], out_hbm.at[:, x], osem.at[slot])

    @pl.loop(0, items)
    def _(i):
        slot = i & 1
        if outer:
            for j in range(3):
                arrive(3 * i + j)
        else:
            @pl.when(i == 0)
            def _():
                arrive(0)
                arrive(1)
            arrive(i + 2)

        engine.layer(i, 1 + stride * i)

        @pl.when(i > 1)
        def _():
            write(i - 2, slot).wait()

        engine.finish(slot)
        write(i, slot).start()

    for i in range(max(items - 2, 0), items):
        write(i, i & 1).wait()


def layers(weights, coefs, fields, halos=None, out=None):
    outer = halos is not None
    terms, nx, ny, nz = coefs.shape
    outs, depth = weights.shape
    total = depth // terms
    sources = len(fields)
    block = block_of(outs)
    items = 2 if outer else nx - 2
    slots = 6 if outer else nx
    shape = jax.ShapeDtypeStruct((outs, nx, ny, nz), BF16)
    operands = [weights, coefs, *fields] + ([*halos[0], *halos[1], out] if outer else [])
    scratch = engine_scratch(slots, items, terms, ny, nz, total, outs, block)
    scratch.append(pltpu.VMEM((slots, ny, total, nz), BF16))
    more = []
    if outer:
        more = [pltpu.VMEM((2, ny, extra_of(terms, ny), nz), BF16), pltpu.SemaphoreType.DMA((2,))]
    return pl.pallas_call(
        functools.partial(layers_kernel, sources, outer),
        in_specs=[VMEM, VMEM] + [HBM] * (len(operands) - 2),
        out_specs=HBM,
        out_shape=shape,
        input_output_aliases={len(operands) - 1: 0} if outer else {},
        scratch_shapes=[
            *scratch,
            pltpu.SemaphoreType.DMA((sources, slots)),
            pltpu.SemaphoreType.DMA((2,)),
            *more,
        ],
        compiler_params=grant(*scratch, weights, coefs),
        cost_estimate=pl.CostEstimate(
            flops=2 * outs * depth * items * ny * nz, bytes_accessed=6 * 2**20, transcendentals=0
        ),
        name="outer" if outer else "inner",
    )(*operands)


def solution(mesh):
    sources, bricks = mesh.shape[MODE], mesh.shape[GRID]

    def around(block):
        found = [block]
        for r in range(1, sources):
            found.append(lax.ppermute(block, MODE, [((i + r) % sources, i) for i in range(sources)]))
        return found

    def exchange(block, offset):
        pairs = [(i, i + 1) for i in range(offset, bricks - 1, 2)]
        return lax.ppermute(block, GRID, pairs + [(b, a) for a, b in pairs])

    def halves(field, coupling, coefs):
        def swap(block):
            return lax.ppermute(block, MODE, [(0, 1), (1, 0)])

        turned, even_out, odd_out, weights, send = turn(field, coefs, coupling, coefs.shape[1] // 2 + 1)
        weights = (weights, swap(weights))
        even_in, odd_in = exchange(even_out, 0), exchange(odd_out, 1)
        other = swap(send)
        out, give = half_layers(weights, coefs, turned, other)
        even_in, odd_in, out, give = lax.optimization_barrier((even_in, odd_in, out, give))
        inner = swap(give)
        halos = (even_in, swap(even_in), odd_in, swap(odd_in))
        out, give = half_layers(weights, coefs, turned, other, halos, (out,))
        return join(inner, swap(give), out)

    def body(field, coupling, coefs):
        if sources == 2 and coefs.shape[1] % 2 == 0 and coefs.shape[1] >= 4:
            return halves(field, coupling, coefs)
        turned, even_out, odd_out, weights = turn(field, coefs, coupling)
        even_in, odd_in = exchange(even_out, 0), exchange(odd_out, 1)
        fields = around(turned)
        out = layers(weights, coefs, fields)
        even_in, odd_in, out = lax.optimization_barrier((even_in, odd_in, out))
        return layers(weights, coefs, fields, (around(even_in), around(odd_in)), out)

    spec = P(MODE, GRID, None, None)
    return jax.shard_map(
        body,
        mesh=mesh,
        in_specs=(spec, P(None, MODE, None), P(None, GRID, None, None)),
        out_specs=spec,
        check_vma=False,
    )
```
